256 devices in a mesh: seq: 32 (over y, x, core), exp: 8 (over z).
Axes of the slice: x: 4, y: 4, z: 8, core: 2. Of those that a mesh axis runs over, the one named last changes fastest.
Arguments:
- queries: bfloat16 [4096, 7168], P('seq', 'exp'), may hold values from -8 to 8
- keys: bfloat16 [4096, 7168], P('seq', 'exp'), may hold values from -8 to 8
- values: bfloat16 [4096, 7168], P('seq', 'exp'), may hold values from -34 to 34
- branch_gates: float32 [4096, 2, 56], P('seq', None, 'exp'), may hold values from 0.1 to 1
- block_choice: int32 [64, 8], P('seq'), may hold values from 0 to 14, as said below
- norm_gain: float32 [7168], P('exp'), may hold values from 0.5 to 1.5
- expert_ids: int32 [4096, 8], P('seq'), may hold values from 0 to 31, all different within a row; in each aligned block of 128 rows (0 to 127, 128 to 255, ...) at most 40 rows name the same one
- route_scores: float32 [4096, 8], P('seq'), may hold values from 0.05 to 1
- w_gate_up: bfloat16 [32, 7168, 2, 1536], P('seq', 'exp'), may hold values from -0.0625 to 0.0625
- w_down: bfloat16 [32, 1536, 7168], P('seq', None, 'exp'), may hold values from -0.15625 to 0.15625
Outputs:
- mixed: bfloat16 [4096, 7168], P('seq', 'exp')
The draws below stay inside these ranges and needn't reach their ends.
Inputs may be any that keep to these rules, and one draw needn't show every extreme that they name: `block_choice`: each row holds offset 0 and 7 other distinct offsets. `expert_ids`: each row names 8 different experts; within each aligned block of 128 rows (the rows of one index of seq) no expert is named more than 40 times, and that many is reached.
All inputs are finite; a program needn't handle non-finite values.
Results may differ from the reference program's by a relative error of at most 0.029.
Values may be sent and summed in bfloat16 or wider, within the bound.
No kernel may reach another device: no remote copies, remote signals or barrier semaphores. Data moves between devices by JAX's collectives and lax.ppermute only.
A program may use at most 128 MiB of HBM per device.

```python
import math
import jax
import jax.numpy as jnp
import numpy as np
from jax import lax

TOK_SEQ = 128
HEADS = 56
HD = 128
D = 7168
H = 1536
TOPK = 8
BLOCK = 64
TOPSEL = 8
WINDOW = 15
EXPERTS = 32
SEQ_LEN = 4096
NBLK = 64
CAP = 40
N_SEQ = 32
N_EXP = 8


def draw_queries(key, part):
    normal_part = jnp.clip(jax.random.normal(jax.random.fold_in(key, 1), (SEQ_LEN, D), jnp.float32), -3.0, 3.0)
    return normal_part.astype(jnp.bfloat16)


def draw_keys(key, part):
    normal_part = jnp.clip(jax.random.normal(jax.random.fold_in(key, 2), (SEQ_LEN, D), jnp.float32), -3.0, 3.0)
    return normal_part.astype(jnp.bfloat16)


def draw_values(key, part):
    normal_part = jnp.clip(jax.random.normal(jax.random.fold_in(key, 3), (SEQ_LEN, D), jnp.float32), -3.0, 3.0)
    jitter = jnp.exp(jax.random.uniform(jax.random.fold_in(key, 4), (HEADS,), jnp.float32, -0.22, 0.22))
    largest = 3.0
    head_scale = largest ** (jnp.arange(HEADS, dtype=jnp.float32) / (HEADS - 1)) * jitter
    shaped = normal_part.reshape(SEQ_LEN, HEADS, HD) * head_scale[None, :, None]
    return shaped.reshape(SEQ_LEN, D).astype(jnp.bfloat16)


def draw_block_choice(key, part):
    scores = jax.random.randint(jax.random.fold_in(key, 5), (NBLK, WINDOW - 1), 0, 1 << 20) * (WINDOW - 1) + jnp.arange(WINDOW - 1, dtype=jnp.int32)[None, :]
    ranking = jnp.argsort(scores, axis=1)
    others = ranking[:, :TOPSEL - 1] + 1
    return jnp.concatenate([jnp.zeros((NBLK, 1), jnp.int32), others.astype(jnp.int32)], axis=1)


def levels(key, shape, cuts, low, top_value):
    def one(position, parts):
        steps = jax.random.uniform(jax.random.fold_in(jax.random.fold_in(key, 6), position), (parts,), jnp.float32, low / len(cuts), top_value / len(cuts))
        return jnp.repeat(jnp.exp(steps), shape[position] // parts).reshape((-1,) + (1,) * (len(shape) - position - 1))

    loudness = one(*cuts[0])
    for cut in cuts[1:]:
        loudness = loudness * one(*cut)
    return loudness


def deal_out(key, own, number, rows, amount, top, most, skew):
    sequence = jax.random.permutation(key, amount)
    heavy_load, common = portions_of(amount, rows * top, most, skew, True), portions_of(amount, rows * top, most, skew, False)
    places = jnp.arange(amount)

    def named(sizes, rotation):
        used = int((sizes > 0).sum())
        fixed = max(1, used // 4)
        moved = fixed + (places - fixed + rotation * (used - fixed)) % max(1, amount - fixed)
        return jnp.zeros((amount,), jnp.int32).at[sequence[jnp.where(places < fixed, places, moved)]].set(jnp.asarray(sizes, jnp.int32))

    sizes = jnp.where(number % 4 == 0, named(heavy_load, number // 4), named(common, number - number // 4 - 1))
    mixed = jax.random.permutation(jax.random.fold_in(own, 3), amount)
    source_of, receiver = mixed[0:amount // 2 * 2:2], mixed[1:amount // 2 * 2:2]
    room = jnp.minimum(sizes[source_of] - 1, most - sizes[receiver]) // 2
    room = jnp.where((source_of == sequence[0]) | (receiver == sequence[0]) | (sizes[receiver] == 0), 0, jnp.maximum(room, 0))
    moved = jax.random.randint(jax.random.fold_in(own, 4), (amount // 2,), 0, 1 << 20) % (room + 1)
    sizes = sizes.at[source_of].add(-moved).at[receiver].add(moved)
    members = jnp.searchsorted(jnp.cumsum(sizes), jnp.arange(rows * top), side="right").astype(jnp.int32)
    listing = members.reshape(top, rows).T
    listing = listing[jax.random.permutation(jax.random.fold_in(own, 1), rows)]
    rotation = jax.random.randint(jax.random.fold_in(own, 2), (rows, 1), 0, top)
    return jnp.take_along_axis(listing, (jnp.arange(top)[None, :] + rotation) % top, axis=1)


def portions_of(number_of, total, reach, lean, full):
    portions = [(1 << 20) // math.isqrt(rank ** lean) + 1 for rank in range(1, number_of + 1)]
    largest = reach if full else min(reach, max(-(-total // number_of), total * portions[0] // sum(portions)))
    least = 1 if total - largest >= number_of - 1 else 0
    counts, rest = [largest] + [least] * (number_of - 1), total - largest - least * (number_of - 1)
    while rest > 0:
        free = [i for i in range(1, number_of) if counts[i] < largest] or [i for i in range(1, number_of) if counts[i] < reach]
        whole, remaining = sum([portions[i] for i in free]), rest
        for i in free:
            more = min(reach - counts[i], max(1, remaining * portions[i] // whole), rest)
            counts[i] = counts[i] + more
            rest = rest - more
    return np.array(counts)


def noise(own_key, extent, deviation, reach, shards=(), held_as=jnp.bfloat16):
    result = jax.random.normal(own_key, extent, jnp.float32) * deviation
    if len(shards) > 0:
        result = levels(own_key, extent, shards, -0.22, 0.18) * result
    return jnp.clip(result, min=-reach, max=reach).astype(held_as)


def setup_inputs(seed: int = 0) -> dict:
    streams_of = jax.random.split(jax.random.key(seed), 11)
    queries = draw_queries(jax.random.fold_in(streams_of[10], 71), 0)
    keys = draw_keys(jax.random.fold_in(streams_of[10], 71), 0)
    values = draw_values(jax.random.fold_in(streams_of[10], 71), 0)
    branch_gates = jnp.clip(0.1 + 0.9 * jax.random.uniform(streams_of[3], (SEQ_LEN, 2, HEADS), jnp.float32) ** levels(streams_of[3], (SEQ_LEN, 2, HEADS), ((0, 32), (2, 8)), -0.2, 0.2), 0.1, 1.0)
    block_choice = draw_block_choice(jax.random.fold_in(streams_of[10], 71), 0)
    norm_gain = jnp.clip(1.0 + 0.1 * jax.random.normal(streams_of[5], (D,), jnp.float32), 0.5, 1.5)
    expert_ids_keys = jax.random.split(jax.random.fold_in(streams_of[6], 1), SEQ_LEN // TOK_SEQ)
    expert_ids_turns = jax.random.permutation(jax.random.fold_in(streams_of[6], 3), SEQ_LEN // TOK_SEQ)
    expert_ids = jax.vmap(lambda own, number: deal_out(jax.random.fold_in(streams_of[6], 2), own, number, TOK_SEQ, EXPERTS, TOPK, CAP, 2))(expert_ids_keys, expert_ids_turns).reshape((SEQ_LEN, TOPK))
    route_scores = jnp.clip(jnp.exp(math.log(1.0) - 2.9957323 * jax.random.uniform(streams_of[7], (SEQ_LEN, TOPK), jnp.float32) ** levels(streams_of[7], (SEQ_LEN, TOPK), ((0, 32),), -0.2, 0.2)), 0.05, 1.0)
    w_gate_up = noise(streams_of[8], (EXPERTS, D, 2, H), D ** -0.5, 0.0625, ((0, 32), (1, 8)))
    w_down = noise(streams_of[9], (EXPERTS, H, D), H ** -0.5, 0.15625, ((0, 32), (2, 8)))
    return dict(queries=queries, keys=keys, values=values, branch_gates=branch_gates, block_choice=block_choice, norm_gain=norm_gain, expert_ids=expert_ids, route_scores=route_scores, w_gate_up=w_gate_up, w_down=w_down)


EPSILON = 1e-06
ROUTE_SCALE = 2.5
MASKED_SCORE = -1e+30

def rounded(x):
    return lax.optimization_barrier(x.astype(jnp.bfloat16)).astype(jnp.float32)

def coarse_branch(query_heads, pooled_keys, pooled_values, score_scale):
    seq_len = query_heads.shape[0]
    blocks = pooled_keys.shape[0]
    scores = jnp.einsum('qhd,chd->hqc', query_heads.astype(jnp.float32), pooled_keys.astype(jnp.float32)) * score_scale
    earlier = jnp.arange(blocks, dtype=jnp.int32)[None, :] < (jnp.arange(seq_len, dtype=jnp.int32) // BLOCK)[:, None]
    masked = jnp.where(earlier[None], scores, MASKED_SCORE)
    row_max = lax.optimization_barrier(jnp.max(masked, axis=2, keepdims=True))
    row_max = jnp.where(row_max > 0.5 * MASKED_SCORE, row_max, 0.0)
    weights = jnp.where(earlier[None], jnp.exp(scores - row_max), 0.0)
    weight_sum = lax.optimization_barrier(jnp.sum(weights, axis=2))
    numerator = jnp.einsum('hqc,chd->hqd', rounded(weights), pooled_values.astype(jnp.float32))
    return numerator / jnp.maximum(weight_sum, 1.0)[..., None]

def fine_branch(query_heads, key_heads, value_heads, block_choice, score_scale):
    seq_len = query_heads.shape[0]
    blocks = seq_len // BLOCK
    within = jnp.arange(BLOCK, dtype=jnp.int32)

    def one_block(block_index):
        query_rows = lax.dynamic_slice_in_dim(query_heads, block_index * BLOCK, BLOCK, 0).astype(jnp.float32)
        key_blocks = block_index - block_choice[block_index]
        reachable = key_blocks >= 0
        starts = (jnp.maximum(key_blocks, 0) * BLOCK).astype(jnp.int32)
        key_picked = jax.vmap(lambda start_row: lax.dynamic_slice_in_dim(key_heads, start_row, BLOCK, 0))(starts).astype(jnp.float32)
        value_picked = jax.vmap(lambda start_row: lax.dynamic_slice_in_dim(value_heads, start_row, BLOCK, 0))(starts).astype(jnp.float32)
        scores = jnp.einsum('qhd,skhd->hqsk', query_rows, key_picked) * score_scale
        key_pos = key_blocks[:, None] * BLOCK + within[None, :]
        query_pos = block_index * BLOCK + within
        allowed = reachable[None, :, None] & (key_pos[None, :, :] <= query_pos[:, None, None])
        masked = jnp.where(allowed[None], scores, MASKED_SCORE)
        row_max = lax.optimization_barrier(jnp.max(masked, axis=(2, 3), keepdims=True))
        weights = jnp.where(allowed[None], jnp.exp(scores - row_max), 0.0)
        weight_sum = lax.optimization_barrier(jnp.sum(weights, axis=(2, 3)))
        numerator = jnp.einsum('hqsk,skhd->hqd', rounded(weights), value_picked)
        return numerator / weight_sum[..., None]
    per_block = lax.map(one_block, jnp.arange(blocks, dtype=jnp.int32))
    return jnp.transpose(per_block, (1, 0, 2, 3)).reshape(HEADS, seq_len, HD)

def reference(queries, keys, values, branch_gates, block_choice, norm_gain, expert_ids, route_scores, w_gate_up, w_down):
    seq_len = queries.shape[0]
    blocks = seq_len // BLOCK
    score_scale = HD ** (-0.5)
    query_heads = queries.reshape(seq_len, HEADS, HD)
    key_heads = keys.reshape(seq_len, HEADS, HD)
    value_heads = values.reshape(seq_len, HEADS, HD)
    pooled_keys = lax.optimization_barrier(jnp.mean(keys.astype(jnp.float32).reshape(blocks, BLOCK, D), axis=1)).astype(jnp.bfloat16)
    pooled_values = lax.optimization_barrier(jnp.mean(values.astype(jnp.float32).reshape(blocks, BLOCK, D), axis=1)).astype(jnp.bfloat16)
    coarse_out = coarse_branch(query_heads, pooled_keys.reshape(blocks, HEADS, HD), pooled_values.reshape(blocks, HEADS, HD), score_scale)
    fine_out = fine_branch(query_heads, key_heads, value_heads, block_choice, score_scale)
    gate_coarse = jnp.transpose(branch_gates[:, 0, :])[..., None]
    gate_fine = jnp.transpose(branch_gates[:, 1, :])[..., None]
    joined = gate_coarse * coarse_out + gate_fine * fine_out
    attended = jnp.transpose(joined, (1, 0, 2)).reshape(seq_len, D).astype(jnp.bfloat16)
    wide_rows = attended.astype(jnp.float32)
    square_parts = lax.optimization_barrier(jnp.sum((wide_rows * wide_rows).reshape(seq_len, N_EXP, D // N_EXP), axis=2))
    square_sum = lax.optimization_barrier(jnp.sum(rounded(square_parts), axis=1))
    inverse_rms = lax.rsqrt(square_sum / D + EPSILON)
    normed = (wide_rows * norm_gain).astype(jnp.bfloat16)
    route_weight = ROUTE_SCALE * route_scores / lax.optimization_barrier(jnp.sum(route_scores, axis=1, keepdims=True))
    routes = expert_ids.reshape(N_SEQ, TOK_SEQ * TOPK)
    onehot = (routes[:, :, None] == jnp.arange(EXPERTS, dtype=jnp.int32)[None, None, :]).astype(jnp.int32)
    running = jnp.cumsum(onehot, axis=1) - 1
    slot_index = lax.optimization_barrier(jnp.sum(running * onehot, axis=2)).astype(jnp.int32)
    sources = jnp.broadcast_to(jnp.arange(N_SEQ, dtype=jnp.int32)[:, None], routes.shape)
    token_index = sources * TOK_SEQ + (jnp.arange(TOK_SEQ * TOPK, dtype=jnp.int32) // TOPK)[None, :]
    slot_table = jnp.full((EXPERTS, N_SEQ, CAP), -1, jnp.int32).at[routes, sources, slot_index].set(token_index)
    weight_table = jnp.zeros((EXPERTS, N_SEQ, CAP), jnp.float32).at[routes, sources, slot_index].set(route_weight.reshape(N_SEQ, TOK_SEQ * TOPK))

    def expert_step(routed, expert_index):
        row_index = slot_table[expert_index].reshape(-1)
        filled = row_index >= 0
        clamped = jnp.maximum(row_index, 0)
        picked = normed[clamped].astype(jnp.float32).reshape(-1, N_EXP, D // N_EXP)
        weight_rows = w_gate_up[expert_index].astype(jnp.float32).reshape(N_EXP, D // N_EXP, 2, H)
        partials = jnp.einsum('rnd,ndgh->rngh', picked, weight_rows)
        summed = lax.optimization_barrier(jnp.sum(rounded(partials), axis=1))
        row_scale = inverse_rms[clamped][:, None]
        activated = (jax.nn.silu(summed[:, 0] * row_scale) * (summed[:, 1] * row_scale)).astype(jnp.bfloat16)
        expert_out = rounded(jnp.dot(activated, w_down[expert_index], preferred_element_type=jnp.float32))
        row_weight = jnp.where(filled, weight_table[expert_index].reshape(-1), 0.0)
        routed = routed.at[clamped].add(row_weight[:, None] * expert_out)
        return (routed, None)
    routed, _ = lax.scan(expert_step, jnp.zeros((seq_len, D), jnp.float32), jnp.arange(EXPERTS, dtype=jnp.int32))
    return (wide_rows + routed).astype(jnp.bfloat16)
```

```python
import functools

import jax
import jax.numpy as jnp
from jax import lax
from jax.experimental import pallas as pl
from jax.experimental.pallas import tpu as pltpu
from jax.sharding import PartitionSpec as P

HD = 128
D = 7168
BLOCK = 64
EPSILON = 1e-06
ROUTE_SCALE = 2.5
MASKED = -1e30
SLOTS = (16, 24)
SUB = 8

f32 = jnp.float32
bf16 = jnp.bfloat16


def mm(a, b, ca, cb):
    return lax.dot_general(a, b, (((ca,), (cb,)), ((), ())), preferred_element_type=f32)


def attention_kernel(
    meta, chosen, ids, route_w, gates, q, *refs, pieces, slots, experts, tokens, heads
):
    kv = refs[:pieces]
    pooled = refs[pieces]
    att_out, slot_out, weight_out = refs[pieces + 1 : pieces + 4]
    x_outs = refs[pieces + 4 : pieces + 4 + len(slots)]
    bias, cbias, onehot = refs[pieces + 4 + len(slots) :]
    h = pl.program_id(0)
    row = meta[0]
    blocks_here = tokens // BLOCK
    all_blocks = cbias.shape[1]
    scale = HD ** (-0.5)

    @pl.when(h == 0)
    def _():
        q_in = lax.broadcasted_iota(jnp.int32, (tokens, tokens), 0)
        k_in = lax.broadcasted_iota(jnp.int32, (tokens, tokens), 1)
        gap = q_in // BLOCK - k_in // BLOCK
        for p in range(pieces):
            delta = meta[1 + p]
            offset = gap + blocks_here * delta
            hit = offset == chosen[:, 0:1]
            for j in range(1, chosen.shape[1]):
                hit = hit | (offset == chosen[:, j : j + 1])
            ok = hit & (row >= delta)
            if p == 0:
                ok = ok & (k_in <= q_in)
            bias[:, p * tokens : (p + 1) * tokens] = jnp.where(ok, 0.0, MASKED)
        cq = lax.broadcasted_iota(jnp.int32, (tokens, all_blocks), 0) // BLOCK + row * blocks_here
        cb = lax.broadcasted_iota(jnp.int32, (tokens, all_blocks), 1)
        cbias[...] = jnp.where(cb < cq, 0.0, MASKED)
        expert = lax.broadcasted_iota(jnp.int32, (experts, tokens), 0)
        named = jnp.zeros((experts, tokens), f32)
        weight = jnp.zeros((experts, tokens), f32)
        for k in range(ids.shape[0]):
            same = expert == ids[k : k + 1, :]
            named = jnp.where(same, 1.0, named)
            weight = jnp.where(same, route_w[k : k + 1, :], weight)
        before = jnp.where(q_in < k_in, 1.0, 0.0).astype(bf16)
        count = mm(named.astype(bf16), before, 1, 0)
        slot = jnp.where(named > 0.5, count, -1.0)
        slot_out[...] = slot
        weight_out[...] = weight
        base = 0
        for s in slots:
            at = (lax.broadcasted_iota(jnp.int32, (experts, s, tokens), 1) + base).astype(f32)
            hot = jnp.where(slot[:, None, :] == at, 1.0, 0.0)
            onehot[base * experts : (base + s) * experts, :] = hot.reshape(
                experts * s, tokens
            ).astype(bf16)
            base += s

    qh = q[...]
    scores = [mm(qh, kv[p][0], 1, 1) for p in range(pieces)]
    s = jnp.concatenate(scores, axis=1) * scale + bias[...]
    top = jnp.max(s, axis=1, keepdims=True)
    w = jnp.exp(s - top)
    total = jnp.sum(w, axis=1, keepdims=True)
    wb = w.astype(bf16)
    fine = mm(wb[:, :tokens], kv[0][1], 1, 0)
    for p in range(1, pieces):
        fine = fine + mm(wb[:, p * tokens : (p + 1) * tokens], kv[p][1], 1, 0)
    fine = fine / total
    cs = mm(qh, pooled[0], 1, 1) * scale + cbias[...]
    ctop = jnp.max(cs, axis=1, keepdims=True)
    ctop = jnp.where(ctop > 0.5 * MASKED, ctop, 0.0)
    cw = jnp.exp(cs - ctop)
    ctotal = jnp.sum(cw, axis=1, keepdims=True)
    coarse = mm(cw.astype(bf16), pooled[1], 1, 0) / jnp.maximum(ctotal, 1.0)
    lane = lax.broadcasted_iota(jnp.int32, gates.shape, 1)
    gate_c = jnp.sum(jnp.where(lane == h, gates[...], 0.0), axis=1, keepdims=True)
    gate_f = jnp.sum(jnp.where(lane == h + heads, gates[...], 0.0), axis=1, keepdims=True)
    att = (gate_c * coarse + gate_f * fine).astype(bf16)
    att_out[...] = att
    base = 0
    for x_out, s in zip(x_outs, slots):
        x_out[...] = mm(
            onehot[base * experts : (base + s) * experts, :], att, 1, 0
        ).astype(bf16)
        base += s


def attention(meta, chosen, ids, route_w, gates, q, kv, pooled, slots, experts):
    tokens, features = q.shape
    heads = features // HD
    pieces = len(kv)
    all_blocks = pooled.shape[1]
    whole = lambda a: pl.BlockSpec(a.shape, lambda h, m: (0,) * a.ndim)
    return pl.pallas_call(
        functools.partial(
            attention_kernel,
            pieces=pieces,
            slots=slots,
            experts=experts,
            tokens=tokens,
            heads=heads,
        ),
        name="attend",
        grid_spec=pltpu.PrefetchScalarGridSpec(
            num_scalar_prefetch=1,
            grid=(heads,),
            in_specs=[whole(chosen), whole(ids), whole(route_w), whole(gates)]
            + [pl.BlockSpec((tokens, HD), lambda h, m: (0, h))]
            + [pl.BlockSpec((2, tokens, HD), lambda h, m: (0, 0, h))] * pieces
            + [pl.BlockSpec((2, all_blocks, HD), lambda h, m: (0, 0, h))],
            out_specs=[pl.BlockSpec((tokens, HD), lambda h, m: (0, h))]
            + [pl.BlockSpec((experts, tokens), lambda h, m: (0, 0))] * 2
            + [pl.BlockSpec((experts * s, HD), lambda h, m: (0, h)) for s in slots],
            scratch_shapes=[
                pltpu.VMEM((tokens, pieces * tokens), f32),
                pltpu.VMEM((tokens, all_blocks), f32),
                pltpu.VMEM((experts * sum(slots), tokens), bf16),
            ],
        ),
        out_shape=[jax.ShapeDtypeStruct((tokens, features), bf16)]
        + [jax.ShapeDtypeStruct((experts, tokens), f32)] * 2
        + [jax.ShapeDtypeStruct((experts * s, features), bf16) for s in slots],
    )(meta, chosen, ids, route_w, gates, q, *kv, pooled)


def project_kernel(w, x, out, square, *, half):
    @pl.when(pl.program_id(0) == 0)
    def _():
        wide = x[...].astype(f32)
        square[...] = mm(
            jnp.ones((SUB, wide.shape[1]), bf16), (wide * wide).astype(bf16), 1, 1
        ).astype(bf16)

    both = mm(w[0], x[...], 1, 1).astype(bf16)
    out[0, :half, :] = both[:half]
    out[0, half : half + SUB, :] = square[...]
    out[0, half + SUB :, :] = both[half:]


def project(w, x):
    shards, width, features = w.shape
    rows = x.shape[0]
    return pl.pallas_call(
        functools.partial(project_kernel, half=width // 2),
        name="project",
        grid=(shards,),
        in_specs=[
            pl.BlockSpec((1, width, features), lambda z: (z, 0, 0)),
            pl.BlockSpec((rows, features), lambda z: (0, 0)),
        ],
        out_specs=pl.BlockSpec((1, width + SUB, rows), lambda z: (z, 0, 0)),
        out_shape=jax.ShapeDtypeStruct((shards, width + SUB, rows), bf16),
        scratch_shapes=[pltpu.VMEM((SUB, rows), bf16)],
    )(w, x)


def activate_kernel(at, right, left, own, out, *, half):
    mine = own[0].astype(f32)
    gate_sq = right[...].astype(f32) + mine[: half + SUB]
    up = left[...].astype(f32) + mine[half + SUB :]
    r = lax.rsqrt(gate_sq[half : half + 1] / D + EPSILON)
    gate = gate_sq[:half] * r
    out[...] = (gate / (1.0 + jnp.exp(-gate)) * (up * r)).astype(bf16)


def activate(at, right, left, parts):
    half, rows = left.shape
    return pl.pallas_call(
        functools.partial(activate_kernel, half=half),
        name="activate",
        grid_spec=pltpu.PrefetchScalarGridSpec(
            num_scalar_prefetch=1,
            grid=(1,),
            in_specs=[
                pl.BlockSpec(right.shape, lambda i, a: (0, 0)),
                pl.BlockSpec(left.shape, lambda i, a: (0, 0)),
                pl.BlockSpec((1, 2 * half + SUB, rows), lambda i, a: (a[0], 0, 0)),
            ],
            out_specs=pl.BlockSpec((half, rows), lambda i, a: (0, 0)),
        ),
        out_shape=jax.ShapeDtypeStruct((half, rows), bf16),
    )(at, right, left, parts)


def down_kernel(places, *refs):
    acts = refs[:-3]
    w, out, joined = refs[-3:]
    half = acts[0].shape[0]
    for k, a in enumerate(acts):
        joined[pl.ds(pl.multiple_of(places[k] * half, 64), half), :] = a[...]
    out[...] = mm(joined[...], w[...], 0, 0).astype(bf16)


def down(places, acts, w, tile=256):
    half, rows = acts[0].shape
    hidden, features = w.shape
    return pl.pallas_call(
        down_kernel,
        name="down",
        grid_spec=pltpu.PrefetchScalarGridSpec(
            num_scalar_prefetch=1,
            grid=(rows // tile,),
            in_specs=[pl.BlockSpec((half, tile), lambda i, a: (0, i))] * len(acts)
            + [pl.BlockSpec((hidden, features), lambda i, a: (0, 0))],
            out_specs=pl.BlockSpec((tile, features), lambda i, a: (i, 0)),
            scratch_shapes=[pltpu.VMEM((hidden, tile), bf16)],
        ),
        out_shape=jax.ShapeDtypeStruct((rows, features), bf16),
    )(places, *acts, w)


def combine_kernel(slot, weight, x, back, out, *, base, slots):
    experts, tokens = slot.shape
    at = (lax.broadcasted_iota(jnp.int32, (experts, slots, tokens), 1) + base).astype(f32)
    hot = jnp.where(slot[...][:, None, :] == at, weight[...][:, None, :], 0.0)
    mix = hot.reshape(experts * slots, tokens).astype(bf16)
    out[...] = (x[...].astype(f32) + mm(mix, back[...], 0, 0)).astype(out.dtype)


def combine(slot, weight, x, back, base, slots, dtype):
    whole = lambda a: pl.BlockSpec(a.shape, lambda i: (0,) * a.ndim)
    return pl.pallas_call(
        functools.partial(combine_kernel, base=base, slots=slots),
        name="combine",
        grid=(1,),
        in_specs=[whole(slot), whole(weight), whole(x), whole(back)],
        out_specs=whole(x),
        out_shape=jax.ShapeDtypeStruct(x.shape, dtype),
    )(slot, weight, x, back)


def added(received, mine):
    return (received.astype(f32) + mine.astype(f32)).astype(bf16)


def local(
    queries,
    keys,
    values,
    branch_gates,
    block_choice,
    norm_gain,
    expert_ids,
    route_scores,
    w_gate_up,
    w_down,
):
    tokens, features = queries.shape
    blocks_here = tokens // BLOCK
    row = lax.axis_index("seq")
    peers = lax.axis_size("seq")
    me = lax.axis_index("exp")
    ring = lax.axis_size("exp")
    hidden = w_down.shape[1]
    half = hidden // ring

    kv = jnp.stack([keys, values])

    def passed(x, by):
        return lax.ppermute(x, "seq", [(i, i + by) for i in range(peers - by)])

    def swapped(x):
        return lax.ppermute(x, "seq", [(i, i ^ 1) for i in range(peers)])

    r2, r4, r6 = passed(kv, 2), passed(kv, 4), passed(kv, 6)
    ra = lax.ppermute(
        kv,
        "seq",
        [(i, i) for i in range(0, peers, 2)] + [(i, i + 8) for i in range(1, peers - 8, 2)],
    )
    pieces = [kv, r2, r4, r6, swapped(ra), swapped(r2), swapped(r4), swapped(r6)]
    odd = row % 2
    meta = jnp.stack(
        [row]
        + [jnp.int32(d) for d in (0, 2, 4, 6)]
        + [jnp.where(odd == 1, 1, 7)]
        + [d + 2 * odd for d in (1, 3, 5)]
    ).astype(jnp.int32)
    pooled_here = jnp.mean(
        kv.astype(f32).reshape(2, blocks_here, BLOCK, features), axis=2
    ).astype(bf16)
    copies = jnp.broadcast_to(pooled_here, (peers, *pooled_here.shape))
    everyone = lax.all_to_all(copies, "seq", split_axis=0, concat_axis=0, tiled=True)
    pooled = jnp.transpose(everyone, (1, 0, 2, 3)).reshape(2, peers * blocks_here, features)
    chosen = jnp.repeat(block_choice, BLOCK, axis=0)
    gates = branch_gates.reshape(tokens, -1)
    route_w = ROUTE_SCALE * route_scores / jnp.sum(route_scores, axis=1, keepdims=True)
    w_up = (
        (w_gate_up[0].astype(f32) * norm_gain[:, None, None])
        .astype(bf16)
        .reshape(features, 2, ring, half)
        .transpose(2, 1, 3, 0)
        .reshape(ring, 2 * half, features)
    )
    att, slot, weight, *xs = attention(
        meta, chosen, expert_ids.T, route_w.T, gates, queries, pieces, pooled, SLOTS, peers
    )

    to_right = [(i, (i + 1) % ring) for i in range(ring)]
    to_left = [(i, (i - 1) % ring) for i in range(ring)]
    send_right = lambda x: lax.ppermute(x, "exp", to_right)
    send_left = lambda x: lax.ppermute(x, "exp", to_left)

    arrived = [
        lax.all_to_all(
            x.reshape(peers, s, features), "seq", split_axis=0, concat_axis=0, tiled=True
        ).reshape(peers * s, features)
        for x, s in zip(xs, SLOTS)
    ]
    order = [0, -1, -2, -3, 1, 2, 3, 4]
    places = jnp.stack([(me + k) % ring for k in order]).astype(jnp.int32)
    mixed = att
    base = 0
    for c, (x, s) in enumerate(zip(arrived, SLOTS)):
        parts = project(w_up, x)

        def piece(k, low, high):
            return lax.dynamic_slice(
                parts, ((me + k) % ring, low, 0), (1, high - low, parts.shape[2])
            )[0]

        right = piece(-1, 0, half + SUB)
        left = piece(1, half + SUB, 2 * half + SUB)
        for step in range(1, ring):
            right = send_right(right)
            left = send_left(left)
            if step < ring - 1:
                right = added(right, piece(-1 - step, 0, half + SUB))
                left = added(left, piece(1 + step, half + SUB, 2 * half + SUB))
        act = activate(places[:1], right, left, parts)
        acts = [act]
        moving = act
        for _ in range(3):
            moving = send_right(moving)
            acts.append(moving)
        moving_right = moving
        moving = act
        for _ in range(3):
            moving = send_left(moving)
            acts.append(moving)
        acts.append(send_right(moving_right) if c % 2 == 0 else send_left(moving))
        result = down(places, acts, w_down[0])
        back = lax.all_to_all(
            result.reshape(peers, s, features), "seq", split_axis=0, concat_axis=0, tiled=True
        ).reshape(peers * s, features)
        last = c == len(SLOTS) - 1
        mixed = combine(slot, weight, mixed, back, base, s, bf16 if last else f32)
        base += s
    return mixed


def solution(mesh):
    placed = (
        P("seq", "exp"),
        P("seq", "exp"),
        P("seq", "exp"),
        P("seq", None, "exp"),
        P("seq", None),
        P("exp"),
        P("seq", None),
        P("seq", None),
        P("seq", "exp", None, None),
        P("seq", None, "exp"),
    )
    return jax.shard_map(
        local, mesh=mesh, in_specs=placed, out_specs=P("seq", "exp"), check_vma=False
    )
```

```python
import functools

import jax
import jax.numpy as jnp
from jax import lax
from jax.experimental import pallas as pl
from jax.experimental.pallas import tpu as pltpu
from jax.sharding import PartitionSpec as P


HD = 128
D = 7168
BLOCK = 64
EPSILON = 1e-06
ROUTE_SCALE = 2.5
MASKED = -1e30
SUB = 8

f32 = jnp.float32
bf16 = jnp.bfloat16


def mm(a, b, ca, cb):
    return lax.dot_general(a, b, (((ca,), (cb,)), ((), ())), preferred_element_type=f32)


def attention_kernel(
    meta, chosen, ids, route_w, gates, q, *refs, pieces, slots, experts, tokens, heads
):
    kv = refs[:pieces]
    pooled = refs[pieces]
    att_out, slot_out, weight_out = refs[pieces + 1 : pieces + 4]
    x_out, bias, cbias, onehot = refs[pieces + 4 :]
    row = meta[0]
    blocks_here = tokens // BLOCK
    all_blocks = cbias.shape[1]
    scale = HD ** (-0.5)

    q_in = lax.broadcasted_iota(jnp.int32, (tokens, tokens), 0)
    k_in = lax.broadcasted_iota(jnp.int32, (tokens, tokens), 1)
    gap = q_in // BLOCK - k_in // BLOCK
    for p in range(pieces):
        delta = meta[1 + p]
        offset = gap + blocks_here * delta
        hit = offset == chosen[:, 0:1]
        for j in range(1, chosen.shape[1]):
            hit = hit | (offset == chosen[:, j : j + 1])
        ok = hit & (row >= delta)
        if p == 0:
            ok = ok & (k_in <= q_in)
        bias[:, p * tokens : (p + 1) * tokens] = jnp.where(ok, 0.0, MASKED)
    cq = lax.broadcasted_iota(jnp.int32, (tokens, all_blocks), 0) // BLOCK + row * blocks_here
    cb = lax.broadcasted_iota(jnp.int32, (tokens, all_blocks), 1)
    cbias[...] = jnp.where(cb < cq, 0.0, MASKED)
    expert = lax.broadcasted_iota(jnp.int32, (experts, tokens), 0)
    named = jnp.zeros((experts, tokens), f32)
    weight = jnp.zeros((experts, tokens), f32)
    for k in range(ids.shape[0]):
        same = expert == ids[k : k + 1, :]
        named = jnp.where(same, 1.0, named)
        weight = jnp.where(same, route_w[k : k + 1, :], weight)
    before = jnp.where(q_in < k_in, 1.0, 0.0).astype(bf16)
    count = mm(named.astype(bf16), before, 1, 0)
    slot = jnp.where(named > 0.5, count, -1.0)
    slot_out[...] = slot
    weight_out[...] = weight
    at = lax.broadcasted_iota(jnp.int32, (experts, slots, tokens), 1).astype(f32)
    hot = jnp.where(slot[:, None, :] == at, 1.0, 0.0)
    onehot[...] = hot.reshape(experts * slots, tokens).astype(bf16)

    for h in range(heads):
        at_h = slice(h * HD, (h + 1) * HD)
        qh = q[:, at_h]
        scores = [mm(qh, kv[p][0, :, at_h], 1, 1) for p in range(pieces)]
        s = jnp.concatenate(scores, axis=1) * scale + bias[...]
        top = jnp.max(s, axis=1, keepdims=True)
        w = jnp.exp(s - top)
        total = jnp.sum(w, axis=1, keepdims=True)
        wb = w.astype(bf16)
        fine = mm(wb[:, :tokens], kv[0][1, :, at_h], 1, 0)
        for p in range(1, pieces):
            fine = fine + mm(wb[:, p * tokens : (p + 1) * tokens], kv[p][1, :, at_h], 1, 0)
        cs = mm(qh, pooled[0, :, at_h], 1, 1) * scale + cbias[...]
        ctop = jnp.max(cs, axis=1, keepdims=True)
        ctop = jnp.where(ctop > 0.5 * MASKED, ctop, 0.0)
        cw = jnp.exp(cs - ctop)
        ctotal = jnp.maximum(jnp.sum(cw, axis=1, keepdims=True), 1.0)
        coarse = mm(cw.astype(bf16), pooled[1, :, at_h], 1, 0)
        att = (
            gates[:, h : h + 1] / ctotal * coarse
            + gates[:, heads + h : heads + h + 1] / total * fine
        ).astype(bf16)
        att_out[:, at_h] = att
        x_out[:, at_h] = mm(onehot[...], att, 1, 0).astype(bf16)


def attention(meta, chosen, ids, route_w, gates, q, kv, pooled, slots, experts):
    tokens, features = q.shape
    pieces = len(kv)
    all_blocks = pooled.shape[1]
    whole = lambda a: pl.BlockSpec(a.shape, lambda i, m: (0,) * len(a.shape))
    ins = [chosen, ids, route_w, gates, q, *kv, pooled]
    outs = [
        jax.ShapeDtypeStruct((tokens, features), bf16),
        jax.ShapeDtypeStruct((experts, tokens), f32),
        jax.ShapeDtypeStruct((experts, tokens), f32),
        jax.ShapeDtypeStruct((experts * slots, features), bf16),
    ]
    return pl.pallas_call(
        functools.partial(
            attention_kernel,
            pieces=pieces,
            slots=slots,
            experts=experts,
            tokens=tokens,
            heads=features // HD,
        ),
        name="attend",
        grid_spec=pltpu.PrefetchScalarGridSpec(
            num_scalar_prefetch=1,
            grid=(1,),
            in_specs=[whole(a) for a in ins],
            out_specs=[whole(a) for a in outs],
            scratch_shapes=[
                pltpu.VMEM((tokens, pieces * tokens), f32),
                pltpu.VMEM((tokens, all_blocks), f32),
                pltpu.VMEM((experts * slots, tokens), bf16),
            ],
        ),
        out_shape=outs,
        compiler_params=pltpu.CompilerParams(vmem_limit_bytes=32 << 20),
    )(meta, *ins)


def begin_kernel(at, gain, x, gate_w, up_w, scaled, square, gate_out, up_out):
    wide = x[...].astype(f32)
    scaled[...] = (wide * gain[...]).astype(bf16)
    square[...] = mm(
        jnp.ones((SUB, x.shape[1]), bf16), (wide * wide).astype(bf16), 1, 1
    ).astype(bf16)
    half = up_out.shape[0]
    gate_out[:half, :] = mm(gate_w[0], scaled[...], 1, 1).astype(bf16)
    gate_out[half:, :] = square[...]
    up_out[...] = mm(up_w[0], scaled[...], 1, 1).astype(bf16)


def begin(at, gain, x, w, shards):
    _, hidden, features = w.shape
    half = hidden // shards
    rows = x.shape[0]
    outs = [
        jax.ShapeDtypeStruct((rows, features), bf16),
        jax.ShapeDtypeStruct((SUB, rows), bf16),
        jax.ShapeDtypeStruct((half + SUB, rows), bf16),
        jax.ShapeDtypeStruct((half, rows), bf16),
    ]
    return pl.pallas_call(
        begin_kernel,
        name="begin",
        grid_spec=pltpu.PrefetchScalarGridSpec(
            num_scalar_prefetch=1,
            grid=(1,),
            in_specs=[
                pl.BlockSpec((1, features), lambda i, a: (0, 0)),
                pl.BlockSpec(x.shape, lambda i, a: (0, 0)),
                pl.BlockSpec((1, half, features), lambda i, a: (0, a[0], 0)),
                pl.BlockSpec((1, half, features), lambda i, a: (1, a[1], 0)),
            ],
            out_specs=[pl.BlockSpec(o.shape, lambda i, a: (0, 0)) for o in outs],
        ),
        out_shape=outs,
    )(at, gain, x, w, w)


def project_kernel(x, square, gate_w, up_w, gate_out, up_out):
    half = up_out.shape[1]
    gate = mm(gate_w[0], x[...], 1, 1).astype(bf16)
    up = mm(up_w[0], x[...], 1, 1).astype(bf16)
    for k in range(up_out.shape[0]):
        gate_out[k, :half, :] = gate[k * half : (k + 1) * half]
        gate_out[k, half:, :] = square[...]
        up_out[k] = up[k * half : (k + 1) * half]


def project(x, square, w, shards, pair=2):
    _, hidden, features = w.shape
    half = hidden // shards
    rows = x.shape[0]
    return pl.pallas_call(
        project_kernel,
        name="project",
        grid=(shards // pair,),
        in_specs=[
            pl.BlockSpec((rows, features), lambda z: (0, 0)),
            pl.BlockSpec((SUB, rows), lambda z: (0, 0)),
            pl.BlockSpec((1, pair * half, features), lambda z: (0, z, 0)),
            pl.BlockSpec((1, pair * half, features), lambda z: (1, z, 0)),
        ],
        out_specs=[
            pl.BlockSpec((pair, half + SUB, rows), lambda z: (z, 0, 0)),
            pl.BlockSpec((pair, half, rows), lambda z: (z, 0, 0)),
        ],
        out_shape=[
            jax.ShapeDtypeStruct((shards, half + SUB, rows), bf16),
            jax.ShapeDtypeStruct((shards, half, rows), bf16),
        ],
    )(x, square, w, w)


def activate_kernel(at, right, left, own_gate, own_up, out):
    half = own_up.shape[1]
    gate_sq = right[...].astype(f32) + own_gate[0].astype(f32)
    up = left[...].astype(f32) + own_up[0].astype(f32)
    r = lax.rsqrt(gate_sq[half : half + 1] / D + EPSILON)
    gate = gate_sq[:half] * r
    out[...] = (gate / (1.0 + jnp.exp(-gate)) * (up * r)).astype(bf16)


def activate(at, right, left, own_gate, own_up):
    _, half, rows = own_up.shape
    return pl.pallas_call(
        activate_kernel,
        name="activate",
        grid_spec=pltpu.PrefetchScalarGridSpec(
            num_scalar_prefetch=1,
            grid=(1,),
            in_specs=[
                pl.BlockSpec(right.shape, lambda i, a: (0, 0)),
                pl.BlockSpec(left.shape, lambda i, a: (0, 0)),
                pl.BlockSpec((1, half + SUB, rows), lambda i, a: (a[0], 0, 0)),
                pl.BlockSpec((1, half, rows), lambda i, a: (a[0], 0, 0)),
            ],
            out_specs=pl.BlockSpec((half, rows), lambda i, a: (0, 0)),
        ),
        out_shape=jax.ShapeDtypeStruct((half, rows), bf16),
    )(at, right, left, own_gate, own_up)


def down_kernel(places, *refs):
    acts, (top, bottom, w, out, joined) = refs[:-5], refs[-5:]
    half = acts[0].shape[0]

    def put(k, offset, a):
        start = pl.multiple_of(places[k] * half + offset, 32)
        joined[pl.ds(start, a.shape[0]), :] = a[...]

    for k, a in enumerate(acts):
        put(k, 0, a)
    put(len(acts), 0, top)
    put(len(acts), top.shape[0], bottom)
    out[...] = mm(joined[...], w[...], 0, 0).astype(bf16)


def down(places, acts, w, tile=256):
    rows = acts[0].shape[1]
    hidden, features = w.shape
    return pl.pallas_call(
        down_kernel,
        name="down",
        grid_spec=pltpu.PrefetchScalarGridSpec(
            num_scalar_prefetch=1,
            grid=(rows // tile,),
            in_specs=[pl.BlockSpec((a.shape[0], tile), lambda i, a: (0, i)) for a in acts]
            + [pl.BlockSpec((hidden, features), lambda i, a: (0, 0))],
            out_specs=pl.BlockSpec((tile, features), lambda i, a: (i, 0)),
            scratch_shapes=[pltpu.VMEM((hidden, tile), bf16)],
        ),
        out_shape=jax.ShapeDtypeStruct((rows, features), bf16),
    )(places, *acts, w)


def combine_kernel(slot, weight, x, back, out, *, slots):
    experts, tokens = slot.shape
    at = lax.broadcasted_iota(jnp.int32, (experts, slots, tokens), 1).astype(f32)
    hot = jnp.where(slot[...][:, None, :] == at, weight[...][:, None, :], 0.0)
    mix = hot.reshape(experts * slots, tokens).astype(bf16)
    out[...] = (x[...].astype(f32) + mm(mix, back[...], 0, 0)).astype(out.dtype)


def combine(slot, weight, x, back, slots):
    whole = lambda a: pl.BlockSpec(a.shape, lambda i: (0,) * a.ndim)
    return pl.pallas_call(
        functools.partial(combine_kernel, slots=slots),
        name="combine",
        grid=(1,),
        in_specs=[whole(slot), whole(weight), whole(x), whole(back)],
        out_specs=whole(x),
        out_shape=jax.ShapeDtypeStruct(x.shape, bf16),
    )(slot, weight, x, back)


def added(received, mine):
    return (received.astype(f32) + mine.astype(f32)).astype(bf16)


def local(
    queries,
    keys,
    values,
    branch_gates,
    block_choice,
    norm_gain,
    expert_ids,
    route_scores,
    w_gate_up,
    w_down,
):
    tokens, features = queries.shape
    blocks_here = tokens // BLOCK
    row = lax.axis_index("seq")
    peers = lax.axis_size("seq")
    me = lax.axis_index("exp")
    ring = lax.axis_size("exp")
    hidden = w_down.shape[1]
    half = hidden // ring

    kv = jnp.stack([keys, values])

    across = 2 * 4
    chip = (row % across) // 2
    odd = row % 2

    def shifted(x, by):
        pairs = [(i, i - i % across + (i + 2 * by) % across) for i in range(peers)]
        return lax.ppermute(x, "seq", pairs)

    def swapped(x):
        return lax.ppermute(x, "seq", [(i, i ^ 1) for i in range(peers)])

    above = lax.ppermute(kv, "seq", [(i, i + across) for i in range(peers - across)])
    far = [shifted(jnp.where(chip >= 4 - by, above, kv), by) for by in (1, 2, 3)]
    beside = swapped(jnp.where(odd == 1, above, kv))
    pieces = [kv, *far, beside, *[swapped(x) for x in far]]
    meta = jnp.stack(
        [row]
        + [jnp.int32(d) for d in (0, 2, 4, 6)]
        + [jnp.where(odd == 1, 1, 7)]
        + [d + 2 * odd for d in (1, 3, 5)]
    ).astype(jnp.int32)
    pooled_here = jnp.mean(
        kv.astype(f32).reshape(2, blocks_here, BLOCK, features), axis=2
    ).astype(bf16)
    copies = jnp.broadcast_to(pooled_here, (peers, *pooled_here.shape))
    everyone = lax.all_to_all(copies, "seq", split_axis=0, concat_axis=0, tiled=True)
    pooled = jnp.transpose(everyone, (1, 0, 2, 3)).reshape(2, peers * blocks_here, features)
    chosen = jnp.repeat(block_choice, BLOCK, axis=0)
    gates = branch_gates.reshape(tokens, -1)
    route_w = ROUTE_SCALE * route_scores / jnp.sum(route_scores, axis=1, keepdims=True)
    w_up = jnp.transpose(w_gate_up[0], (1, 2, 0))
    gain = norm_gain[None, :]
    slots = 5 * tokens * expert_ids.shape[1] // (4 * peers)
    att, slot, weight, x = attention(
        meta, chosen, expert_ids.T, route_w.T, gates, queries, pieces, pooled, slots, peers
    )

    to_right = [(i, (i + 1) % ring) for i in range(ring)]
    to_left = [(i, (i - 1) % ring) for i in range(ring)]
    send_right = lambda x: lax.ppermute(x, "exp", to_right)
    send_left = lambda x: lax.ppermute(x, "exp", to_left)

    arrived = lax.all_to_all(
        x.reshape(peers, slots, features), "seq", split_axis=0, concat_axis=0, tiled=True
    ).reshape(peers * slots, features)
    order = [0, -1, -2, -3, 1, 2, 3, 4]
    places = jnp.stack([(me + k) % ring for k in order]).astype(jnp.int32)
    beginning = jnp.stack([(me - 1) % ring, (me + 1) % ring]).astype(jnp.int32)
    scaled, square, right, left = begin(beginning, gain, arrived, w_up, ring)
    gates_all, ups_all = project(scaled, square, w_up, ring)

    def piece(whole, k):
        return lax.dynamic_slice(whole, ((me + k) % ring, 0, 0), (1, *whole.shape[1:]))[0]

    for step in range(1, ring):
        right, left = send_right(right), send_left(left)
        if step < ring - 1:
            right = added(right, piece(gates_all, -1 - step))
            left = added(left, piece(ups_all, 1 + step))
    act = activate(places[:1], right, left, gates_all, ups_all)
    rights, lefts = [act], [act]
    for _ in range(3):
        rights.append(send_right(rights[-1]))
        lefts.append(send_left(lefts[-1]))
    middle = half // 2
    top, bottom = send_right(rights[-1][:middle]), send_left(lefts[-1][middle:])
    result = down(places, [*rights, *lefts[1:], top, bottom], w_down[0])
    back = lax.all_to_all(
        result.reshape(peers, slots, features), "seq", split_axis=0, concat_axis=0, tiled=True
    ).reshape(peers * slots, features)
    return combine(slot, weight, att, back, slots)


def solution(mesh):
    placed = (
        P("seq", "exp"),
        P("seq", "exp"),
        P("seq", "exp"),
        P("seq", None, "exp"),
        P("seq", None),
        P("exp"),
        P("seq", None),
        P("seq", None),
        P("seq", "exp", None, None),
        P("seq", None, "exp"),
    )

    return jax.shard_map(
        local, mesh=mesh, in_specs=placed, out_specs=P("seq", "exp"), check_vma=False
    )
```

```python
import functools

import jax
import jax.numpy as jnp
from jax import lax
from jax.experimental import pallas as pl
from jax.experimental.pallas import tpu as pltpu
from jax.sharding import PartitionSpec as P


HD = 128
D = 7168
BLOCK = 64
EPSILON = 1e-06
ROUTE_SCALE = 2.5
MASKED = -1e30
SUB = 8
PARTS = (24, 16)

f32 = jnp.float32
bf16 = jnp.bfloat16


def mm(a, b, ca, cb):
    return lax.dot_general(a, b, (((ca,), (cb,)), ((), ())), preferred_element_type=f32)


def attention_kernel(
    meta, chosen, ids, route_w, gates, q, *refs, pieces, slots, experts, tokens, heads
):
    kv = refs[:pieces]
    pooled = refs[pieces]
    att_out, slot_out, weight_out = refs[pieces + 1 : pieces + 4]
    x_outs, (bias, cbias, onehot) = refs[pieces + 4 : -3], refs[-3:]
    row = meta[0]
    blocks_here = tokens // BLOCK
    all_blocks = cbias.shape[1]
    scale = HD ** (-0.5)

    q_in = lax.broadcasted_iota(jnp.int32, (tokens, tokens), 0)
    k_in = lax.broadcasted_iota(jnp.int32, (tokens, tokens), 1)
    gap = q_in // BLOCK - k_in // BLOCK
    for p in range(pieces):
        delta = meta[1 + p]
        offset = gap + blocks_here * delta
        hit = offset == chosen[:, 0:1]
        for j in range(1, chosen.shape[1]):
            hit = hit | (offset == chosen[:, j : j + 1])
        ok = hit & (row >= delta)
        if p == 0:
            ok = ok & (k_in <= q_in)
        bias[:, p * tokens : (p + 1) * tokens] = jnp.where(ok, 0.0, MASKED)
    cq = lax.broadcasted_iota(jnp.int32, (tokens, all_blocks), 0) // BLOCK + row * blocks_here
    cb = lax.broadcasted_iota(jnp.int32, (tokens, all_blocks), 1)
    cbias[...] = jnp.where(cb < cq, 0.0, MASKED)
    expert = lax.broadcasted_iota(jnp.int32, (experts, tokens), 0)
    named = jnp.zeros((experts, tokens), f32)
    weight = jnp.zeros((experts, tokens), f32)
    for k in range(ids.shape[0]):
        same = expert == ids[k : k + 1, :]
        named = jnp.where(same, 1.0, named)
        weight = jnp.where(same, route_w[k : k + 1, :], weight)
    before = jnp.where(q_in < k_in, 1.0, 0.0).astype(bf16)
    count = mm(named.astype(bf16), before, 1, 0)
    slot = jnp.where(named > 0.5, count, -1.0)
    slot_out[...] = slot
    weight_out[...] = weight
    base = 0
    for n in slots:
        at = (lax.broadcasted_iota(jnp.int32, (experts, n, tokens), 1) + base).astype(f32)
        hot = jnp.where(slot[:, None, :] == at, 1.0, 0.0)
        onehot[base * experts : (base + n) * experts, :] = hot.reshape(
            experts * n, tokens
        ).astype(bf16)
        base += n

    for h in range(heads):
        at_h = slice(h * HD, (h + 1) * HD)
        qh = q[:, at_h]
        scores = [mm(qh, kv[p][0, :, at_h], 1, 1) for p in range(pieces)]
        s = jnp.concatenate(scores, axis=1) * scale + bias[...]
        top = jnp.max(s, axis=1, keepdims=True)
        w = jnp.exp(s - top)
        total = jnp.sum(w, axis=1, keepdims=True)
        wb = w.astype(bf16)
        fine = mm(wb[:, :tokens], kv[0][1, :, at_h], 1, 0)
        for p in range(1, pieces):
            fine = fine + mm(wb[:, p * tokens : (p + 1) * tokens], kv[p][1, :, at_h], 1, 0)
        cs = mm(qh, pooled[0, :, at_h], 1, 1) * scale + cbias[...]
        ctop = jnp.max(cs, axis=1, keepdims=True)
        ctop = jnp.where(ctop > 0.5 * MASKED, ctop, 0.0)
        cw = jnp.exp(cs - ctop)
        ctotal = jnp.maximum(jnp.sum(cw, axis=1, keepdims=True), 1.0)
        coarse = mm(cw.astype(bf16), pooled[1, :, at_h], 1, 0)
        att = (
            gates[:, h : h + 1] / ctotal * coarse
            + gates[:, heads + h : heads + h + 1] / total * fine
        ).astype(bf16)
        att_out[:, at_h] = att
        base = 0
        for x_out, n in zip(x_outs, slots):
            rows = slice(base * experts, (base + n) * experts)
            x_out[:, at_h] = mm(onehot[rows, :], att, 1, 0).astype(bf16)
            base += n


def attention(meta, chosen, ids, route_w, gates, q, kv, pooled, slots, experts):
    tokens, features = q.shape
    pieces = len(kv)
    all_blocks = pooled.shape[1]
    whole = lambda a: pl.BlockSpec(a.shape, lambda i, m: (0,) * len(a.shape))
    ins = [chosen, ids, route_w, gates, q, *kv, pooled]
    outs = [
        jax.ShapeDtypeStruct((tokens, features), bf16),
        jax.ShapeDtypeStruct((experts, tokens), f32),
        jax.ShapeDtypeStruct((experts, tokens), f32),
        *[jax.ShapeDtypeStruct((experts * n, features), bf16) for n in slots],
    ]
    return pl.pallas_call(
        functools.partial(
            attention_kernel,
            pieces=pieces,
            slots=slots,
            experts=experts,
            tokens=tokens,
            heads=features // HD,
        ),
        name="attend",
        grid_spec=pltpu.PrefetchScalarGridSpec(
            num_scalar_prefetch=1,
            grid=(1,),
            in_specs=[whole(a) for a in ins],
            out_specs=[whole(a) for a in outs],
            scratch_shapes=[
                pltpu.VMEM((tokens, pieces * tokens), f32),
                pltpu.VMEM((tokens, all_blocks), f32),
                pltpu.VMEM((experts * sum(slots), tokens), bf16),
            ],
        ),
        out_shape=outs,
        compiler_params=pltpu.CompilerParams(vmem_limit_bytes=32 << 20),
    )(meta, *ins)


def project_kernel(gain, x, gate_w, up_w, out, scaled, square):
    half = gate_w.shape[1] // out.shape[0]

    @pl.when(pl.program_id(0) == 0)
    def _():
        wide = x[...].astype(f32)
        scaled[...] = (wide * gain[...]).astype(bf16)
        square[...] = mm(
            jnp.ones((SUB, x.shape[1]), bf16), (wide * wide).astype(bf16), 1, 1
        ).astype(bf16)

    gate = mm(gate_w[0], scaled[...], 1, 1).astype(bf16)
    up = mm(up_w[0], scaled[...], 1, 1).astype(bf16)
    for k in range(out.shape[0]):
        out[k, :half, :] = gate[k * half : (k + 1) * half]
        out[k, half : 2 * half, :] = up[k * half : (k + 1) * half]
        out[k, 2 * half :, :] = square[...]


def project(gain, x, w, shards, pair=2):
    _, hidden, features = w.shape
    half = hidden // shards
    rows = x.shape[0]
    return pl.pallas_call(
        project_kernel,
        name="project",
        grid=(shards // pair,),
        in_specs=[
            pl.BlockSpec((1, features), lambda z: (0, 0)),
            pl.BlockSpec((rows, features), lambda z: (0, 0)),
            pl.BlockSpec((1, pair * half, features), lambda z: (0, z, 0)),
            pl.BlockSpec((1, pair * half, features), lambda z: (1, z, 0)),
        ],
        out_specs=pl.BlockSpec((pair, 2 * half + SUB, rows), lambda z: (z, 0, 0)),
        out_shape=jax.ShapeDtypeStruct((shards, 2 * half + SUB, rows), bf16),
        scratch_shapes=[pltpu.VMEM((rows, features), bf16), pltpu.VMEM((SUB, rows), bf16)],
    )(gain, x, w, w)


def activate_kernel(summed, out):
    half = out.shape[0]
    r = lax.rsqrt(summed[2 * half : 2 * half + 1, :].astype(f32) / D + EPSILON)
    gate = summed[:half, :].astype(f32) * r
    up = summed[half : 2 * half, :].astype(f32) * r
    out[...] = (gate / (1.0 + jnp.exp(-gate)) * up).astype(bf16)


def activate(summed, half):
    rows = summed.shape[1]
    return pl.pallas_call(
        activate_kernel,
        name="activate",
        grid=(1,),
        in_specs=[pl.BlockSpec(summed.shape, lambda i: (0, 0))],
        out_specs=pl.BlockSpec((half, rows), lambda i: (0, 0)),
        out_shape=jax.ShapeDtypeStruct((half, rows), bf16),
    )(summed)


def down_kernel(places, *refs):
    acts, (top, bottom, w, out, joined) = refs[:-5], refs[-5:]
    half = acts[0].shape[0]

    def put(k, offset, a):
        start = pl.multiple_of(places[k] * half + offset, 32)
        joined[pl.ds(start, a.shape[0]), :] = a[...]

    for k, a in enumerate(acts):
        put(k, 0, a)
    put(len(acts), 0, top)
    put(len(acts), top.shape[0], bottom)
    out[...] = mm(joined[...], w[...], 0, 0).astype(bf16)


def down(places, acts, w, tile=256):
    rows = acts[0].shape[1]
    hidden, features = w.shape
    return pl.pallas_call(
        down_kernel,
        name="down",
        grid_spec=pltpu.PrefetchScalarGridSpec(
            num_scalar_prefetch=1,
            grid=(rows // tile,),
            in_specs=[pl.BlockSpec((a.shape[0], tile), lambda i, a: (0, i)) for a in acts]
            + [pl.BlockSpec((hidden, features), lambda i, a: (0, 0))],
            out_specs=pl.BlockSpec((tile, features), lambda i, a: (i, 0)),
            scratch_shapes=[pltpu.VMEM((hidden, tile), bf16)],
        ),
        out_shape=jax.ShapeDtypeStruct((rows, features), bf16),
    )(places, *acts, w)


def combine_kernel(slot, weight, x, back, out, *, base, slots):
    experts, tokens = slot.shape
    at = (lax.broadcasted_iota(jnp.int32, (experts, slots, tokens), 1) + base).astype(f32)
    hot = jnp.where(slot[...][:, None, :] == at, weight[...][:, None, :], 0.0)
    mix = hot.reshape(experts * slots, tokens).astype(bf16)
    out[...] = (x[...].astype(f32) + mm(mix, back[...], 0, 0)).astype(out.dtype)


def combine(slot, weight, x, back, base, slots, dtype):
    whole = lambda a: pl.BlockSpec(a.shape, lambda i: (0,) * a.ndim)
    return pl.pallas_call(
        functools.partial(combine_kernel, base=base, slots=slots),
        name="combine",
        grid=(1,),
        in_specs=[whole(slot), whole(weight), whole(x), whole(back)],
        out_specs=whole(x),
        out_shape=jax.ShapeDtypeStruct(x.shape, dtype),
    )(slot, weight, x, back)


def local(
    queries,
    keys,
    values,
    branch_gates,
    block_choice,
    norm_gain,
    expert_ids,
    route_scores,
    w_gate_up,
    w_down,
):
    tokens, features = queries.shape
    blocks_here = tokens // BLOCK
    row = lax.axis_index("seq")
    peers = lax.axis_size("seq")
    me = lax.axis_index("exp")
    ring = lax.axis_size("exp")
    hidden = w_down.shape[1]
    half = hidden // ring

    kv = jnp.stack([keys, values])

    across = 2 * 4
    chip = (row % across) // 2
    odd = row % 2

    def shifted(x, by):
        pairs = [(i, i - i % across + (i + 2 * by) % across) for i in range(peers)]
        return lax.ppermute(x, "seq", pairs)

    def swapped(x):
        return lax.ppermute(x, "seq", [(i, i ^ 1) for i in range(peers)])

    above = lax.ppermute(kv, "seq", [(i, i + across) for i in range(peers - across)])
    far = [shifted(jnp.where(chip >= 4 - by, above, kv), by) for by in (1, 2, 3)]
    beside = swapped(jnp.where(odd == 1, above, kv))
    pieces = [kv, *far, beside, *[swapped(x) for x in far]]
    meta = jnp.stack(
        [row]
        + [jnp.int32(d) for d in (0, 2, 4, 6)]
        + [jnp.where(odd == 1, 1, 7)]
        + [d + 2 * odd for d in (1, 3, 5)]
    ).astype(jnp.int32)
    pooled_here = jnp.mean(
        kv.astype(f32).reshape(2, blocks_here, BLOCK, features), axis=2
    ).astype(bf16)
    copies = jnp.broadcast_to(pooled_here, (peers, *pooled_here.shape))
    everyone = lax.all_to_all(copies, "seq", split_axis=0, concat_axis=0, tiled=True)
    pooled = jnp.transpose(everyone, (1, 0, 2, 3)).reshape(2, peers * blocks_here, features)
    chosen = jnp.repeat(block_choice, BLOCK, axis=0)
    gates = branch_gates.reshape(tokens, -1)
    route_w = ROUTE_SCALE * route_scores / jnp.sum(route_scores, axis=1, keepdims=True)
    w_up = jnp.transpose(w_gate_up[0], (1, 2, 0))
    gain = norm_gain[None, :]
    att, slot, weight, *xs = attention(
        meta, chosen, expert_ids.T, route_w.T, gates, queries, pieces, pooled, PARTS, peers
    )

    def exchanged(x, n):
        return lax.all_to_all(
            x.reshape(peers, n, features), "seq", split_axis=0, concat_axis=0, tiled=True
        ).reshape(peers * n, features)

    to_right = [(i, (i + 1) % ring) for i in range(ring)]
    to_left = [(i, (i - 1) % ring) for i in range(ring)]
    send_right = lambda x: lax.ppermute(x, "exp", to_right)
    send_left = lambda x: lax.ppermute(x, "exp", to_left)
    order = [0, -1, -2, -3, 1, 2, 3, 4]
    places = jnp.stack([(me + k) % ring for k in order]).astype(jnp.int32)
    middle = half // 2
    summed = []
    for x, n in zip(xs, PARTS):
        whole = project(gain, exchanged(x, n), w_up, ring)
        summed.append(
            lax.psum_scatter(whole.reshape(-1, peers * n), "exp", scatter_dimension=0, tiled=True)
        )
    mixed = att
    base = 0
    for c, n in enumerate(PARTS):
        act = activate(summed[c], half)
        rights, lefts = [act], [act]
        for _ in range(3):
            rights.append(send_right(rights[-1]))
            lefts.append(send_left(lefts[-1]))
        top, bottom = send_right(rights[-1][:middle]), send_left(lefts[-1][middle:])
        result = down(places, [*rights, *lefts[1:], top, bottom], w_down[0])
        back = exchanged(result, n)
        last = c == len(PARTS) - 1
        mixed = combine(slot, weight, mixed, back, base, n, bf16 if last else f32)
        base += n
    return mixed


def solution(mesh):
    placed = (
        P("seq", "exp"),
        P("seq", "exp"),
        P("seq", "exp"),
        P("seq", None, "exp"),
        P("seq", None),
        P("exp"),
        P("seq", None),
        P("seq", None),
        P("seq", "exp", None, None),
        P("seq", None, "exp"),
    )

    return jax.shard_map(
        local, mesh=mesh, in_specs=placed, out_specs=P("seq", "exp"), check_vma=False
    )
```

```python
import functools

import jax
import jax.numpy as jnp
from jax import lax
from jax.experimental import pallas as pl
from jax.experimental.pallas import tpu as pltpu
from jax.sharding import PartitionSpec as P


HD = 128
D = 7168
BLOCK = 64
EPSILON = 1e-06
ROUTE_SCALE = 2.5
MASKED = -1e30
SUB = 8
PARTS = (16, 24)

f32 = jnp.float32
bf16 = jnp.bfloat16


def mm(a, b, ca, cb):
    return lax.dot_general(a, b, (((ca,), (cb,)), ((), ())), preferred_element_type=f32)


def attention_kernel(
    meta, chosen, ids, route_w, gates, q, *refs, pieces, slots, experts, tokens, heads
):
    kv = refs[:pieces]
    pooled = refs[pieces]
    att_out, slot_out, weight_out = refs[pieces + 1 : pieces + 4]
    x_outs, (bias, cbias, onehot) = refs[pieces + 4 : -3], refs[-3:]
    row = meta[0]
    h = pl.program_id(0)
    blocks_here = tokens // BLOCK
    all_blocks = cbias.shape[1]
    scale = HD ** (-0.5)

    @pl.when(h == 0)
    def _():
        q_in = lax.broadcasted_iota(jnp.int32, (tokens, tokens), 0)
        k_in = lax.broadcasted_iota(jnp.int32, (tokens, tokens), 1)
        gap = q_in // BLOCK - k_in // BLOCK
        for p in range(pieces):
            delta = meta[1 + p]
            offset = gap + blocks_here * delta
            hit = offset == chosen[:, 0:1]
            for j in range(1, chosen.shape[1]):
                hit = hit | (offset == chosen[:, j : j + 1])
            ok = hit & (row >= delta)
            if p == 0:
                ok = ok & (k_in <= q_in)
            bias[:, p * tokens : (p + 1) * tokens] = jnp.where(ok, 0.0, MASKED)
        cq = lax.broadcasted_iota(jnp.int32, (tokens, all_blocks), 0) // BLOCK + row * blocks_here
        cb = lax.broadcasted_iota(jnp.int32, (tokens, all_blocks), 1)
        cbias[...] = jnp.where(cb < cq, 0.0, MASKED)
        expert = lax.broadcasted_iota(jnp.int32, (experts, tokens), 0)
        named = jnp.zeros((experts, tokens), f32)
        weight = jnp.zeros((experts, tokens), f32)
        for k in range(ids.shape[0]):
            same = expert == ids[k : k + 1, :]
            named = jnp.where(same, 1.0, named)
            weight = jnp.where(same, route_w[k : k + 1, :], weight)
        before = jnp.where(q_in < k_in, 1.0, 0.0).astype(bf16)
        count = mm(named.astype(bf16), before, 1, 0)
        slot = jnp.where(named > 0.5, count, -1.0)
        slot_out[...] = slot
        weight_out[...] = weight
        base = 0
        for n in slots:
            at = (lax.broadcasted_iota(jnp.int32, (experts, n, tokens), 1) + base).astype(f32)
            hot = jnp.where(slot[:, None, :] == at, 1.0, 0.0)
            onehot[base * experts : (base + n) * experts, :] = hot.reshape(
                experts * n, tokens
            ).astype(bf16)
            base += n

    qh = q[...]
    keys = jnp.concatenate([piece[0] for piece in kv], axis=0)
    s = mm(qh, keys, 1, 1) * scale + bias[...]
    top = jnp.max(s, axis=1, keepdims=True)
    w = jnp.exp(s - top)
    total = jnp.sum(w, axis=1, keepdims=True)
    values = jnp.concatenate([piece[1] for piece in kv], axis=0)
    fine = mm(w.astype(bf16), values, 1, 0)
    cs = mm(qh, pooled[0], 1, 1) * scale + cbias[...]
    ctop = jnp.max(cs, axis=1, keepdims=True)
    ctop = jnp.where(ctop > 0.5 * MASKED, ctop, 0.0)
    cw = jnp.exp(cs - ctop)
    ctotal = jnp.maximum(jnp.sum(cw, axis=1, keepdims=True), 1.0)
    coarse = mm(cw.astype(bf16), pooled[1], 1, 0)
    lane = lax.broadcasted_iota(jnp.int32, gates.shape, 1)
    gate_c = jnp.sum(jnp.where(lane == h, gates[...], 0.0), axis=1, keepdims=True)
    gate_f = jnp.sum(jnp.where(lane == h + heads, gates[...], 0.0), axis=1, keepdims=True)
    att = (gate_c / ctotal * coarse + gate_f / total * fine).astype(bf16)
    att_out[...] = att
    base = 0
    for x_out, n in zip(x_outs, slots):
        rows = slice(base * experts, (base + n) * experts)
        x_out[...] = mm(onehot[rows, :], att, 1, 0).astype(bf16)
        base += n


def attention(meta, chosen, ids, route_w, gates, q, kv, pooled, slots, experts):
    tokens, features = q.shape
    heads = features // HD
    pieces = len(kv)
    all_blocks = pooled.shape[1]

    def whole(a):
        return pl.BlockSpec(a.shape, lambda h, m: (0,) * len(a.shape))

    def per_head(a):
        zeros = (0,) * (len(a.shape) - 1)
        return pl.BlockSpec((*a.shape[:-1], HD), lambda h, m: (*zeros, h))

    small = [chosen, ids, route_w, gates]
    wide = [q, *kv, pooled]
    table = jax.ShapeDtypeStruct((experts, tokens), f32)
    dispatched = [jax.ShapeDtypeStruct((experts * n, features), bf16) for n in slots]
    return pl.pallas_call(
        functools.partial(
            attention_kernel,
            pieces=pieces,
            slots=slots,
            experts=experts,
            tokens=tokens,
            heads=heads,
        ),
        name="attend",
        grid_spec=pltpu.PrefetchScalarGridSpec(
            num_scalar_prefetch=1,
            grid=(heads,),
            in_specs=[whole(a) for a in small] + [per_head(a) for a in wide],
            out_specs=[per_head(q), whole(table), whole(table)]
            + [per_head(a) for a in dispatched],
            scratch_shapes=[
                pltpu.VMEM((tokens, pieces * tokens), f32),
                pltpu.VMEM((tokens, all_blocks), f32),
                pltpu.VMEM((experts * sum(slots), tokens), bf16),
            ],
        ),
        out_shape=[jax.ShapeDtypeStruct((tokens, features), bf16), table, table, *dispatched],
    )(meta, *small, *wide)


def project_kernel(gain, x, gate_w, up_w, out, scaled, square):
    half = gate_w.shape[1] // out.shape[0]

    @pl.when(pl.program_id(0) == 0)
    def _():
        wide = x[...].astype(f32)
        scaled[...] = (wide * gain[...]).astype(bf16)
        square[...] = mm(
            jnp.ones((SUB, x.shape[1]), bf16), (wide * wide).astype(bf16), 1, 1
        ).astype(bf16)

    gate = mm(gate_w[0], scaled[...], 1, 1).astype(bf16)
    up = mm(up_w[0], scaled[...], 1, 1).astype(bf16)
    for k in range(out.shape[0]):
        out[k, :half, :] = gate[k * half : (k + 1) * half]
        out[k, half : 2 * half, :] = up[k * half : (k + 1) * half]
        out[k, 2 * half :, :] = square[...]


def project(gain, x, w, shards, pair=2):
    _, hidden, features = w.shape
    half = hidden // shards
    rows = x.shape[0]
    return pl.pallas_call(
        project_kernel,
        name="project",
        grid=(shards // pair,),
        in_specs=[
            pl.BlockSpec((1, features), lambda z: (0, 0)),
            pl.BlockSpec((rows, features), lambda z: (0, 0)),
            pl.BlockSpec((1, pair * half, features), lambda z: (0, z, 0)),
            pl.BlockSpec((1, pair * half, features), lambda z: (1, z, 0)),
        ],
        out_specs=pl.BlockSpec((pair, 2 * half + SUB, rows), lambda z: (z, 0, 0)),
        out_shape=jax.ShapeDtypeStruct((shards, 2 * half + SUB, rows), bf16),
        scratch_shapes=[pltpu.VMEM((rows, features), bf16), pltpu.VMEM((SUB, rows), bf16)],
    )(gain, x, w, w)


def activate_kernel(summed, out):
    half = out.shape[0]
    r = lax.rsqrt(summed[2 * half : 2 * half + 1, :].astype(f32) / D + EPSILON)
    gate = summed[:half, :].astype(f32) * r
    up = summed[half : 2 * half, :].astype(f32) * r
    out[...] = (gate / (1.0 + jnp.exp(-gate)) * up).astype(bf16)


def activate(summed, half):
    rows = summed.shape[1]
    return pl.pallas_call(
        activate_kernel,
        name="activate",
        grid=(1,),
        in_specs=[pl.BlockSpec(summed.shape, lambda i: (0, 0))],
        out_specs=pl.BlockSpec((half, rows), lambda i: (0, 0)),
        out_shape=jax.ShapeDtypeStruct((half, rows), bf16),
    )(summed)


def down_kernel(places, *refs):
    acts, (top, bottom, w, out, joined) = refs[:-5], refs[-5:]
    half = acts[0].shape[0]

    def put(k, offset, a):
        start = pl.multiple_of(places[k] * half + offset, 32)
        joined[pl.ds(start, a.shape[0]), :] = a[...]

    for k, a in enumerate(acts):
        put(k, 0, a)
    put(len(acts), 0, top)
    put(len(acts), top.shape[0], bottom)
    out[...] = mm(joined[...], w[...], 0, 0).astype(bf16)


def down(places, acts, w, tile=256):
    rows = acts[0].shape[1]
    hidden, features = w.shape
    return pl.pallas_call(
        down_kernel,
        name="down",
        grid_spec=pltpu.PrefetchScalarGridSpec(
            num_scalar_prefetch=1,
            grid=(rows // tile,),
            in_specs=[pl.BlockSpec((a.shape[0], tile), lambda i, a: (0, i)) for a in acts]
            + [pl.BlockSpec((hidden, features), lambda i, a: (0, 0))],
            out_specs=pl.BlockSpec((tile, features), lambda i, a: (i, 0)),
            scratch_shapes=[pltpu.VMEM((hidden, tile), bf16)],
        ),
        out_shape=jax.ShapeDtypeStruct((rows, features), bf16),
    )(places, *acts, w)


def combine_kernel(slot, weight, x, back, out, *, base, slots):
    experts, tokens = slot.shape
    at = (lax.broadcasted_iota(jnp.int32, (experts, slots, tokens), 1) + base).astype(f32)
    hot = jnp.where(slot[...][:, None, :] == at, weight[...][:, None, :], 0.0)
    mix = hot.reshape(experts * slots, tokens).astype(bf16)
    out[...] = (x[...].astype(f32) + mm(mix, back[...], 0, 0)).astype(out.dtype)


def combine(slot, weight, x, back, base, slots, dtype):
    whole = lambda a: pl.BlockSpec(a.shape, lambda i: (0,) * a.ndim)
    return pl.pallas_call(
        functools.partial(combine_kernel, base=base, slots=slots),
        name="combine",
        grid=(1,),
        in_specs=[whole(slot), whole(weight), whole(x), whole(back)],
        out_specs=whole(x),
        out_shape=jax.ShapeDtypeStruct(x.shape, dtype),
    )(slot, weight, x, back)


def local(
    queries,
    keys,
    values,
    branch_gates,
    block_choice,
    norm_gain,
    expert_ids,
    route_scores,
    w_gate_up,
    w_down,
):
    tokens, features = queries.shape
    blocks_here = tokens // BLOCK
    row = lax.axis_index("seq")
    peers = lax.axis_size("seq")
    me = lax.axis_index("exp")
    ring = lax.axis_size("exp")
    hidden = w_down.shape[1]
    half = hidden // ring

    kv = jnp.stack([keys, values])

    across = 2 * 4
    chip = (row % across) // 2
    odd = row % 2

    def shifted(x, by):
        pairs = [(i, i - i % across + (i + 2 * by) % across) for i in range(peers)]
        return lax.ppermute(x, "seq", pairs)

    def swapped(x):
        return lax.ppermute(x, "seq", [(i, i ^ 1) for i in range(peers)])

    above = lax.ppermute(kv, "seq", [(i, i + across) for i in range(peers - across)])
    far = [shifted(jnp.where(chip >= 4 - by, above, kv), by) for by in (1, 2, 3)]
    beside = swapped(jnp.where(odd == 1, above, kv))
    pieces = [kv, *far, beside, *[swapped(x) for x in far]]
    meta = jnp.stack(
        [row]
        + [jnp.int32(d) for d in (0, 2, 4, 6)]
        + [jnp.where(odd == 1, 1, 7)]
        + [d + 2 * odd for d in (1, 3, 5)]
    ).astype(jnp.int32)
    pooled_here = jnp.mean(
        kv.astype(f32).reshape(2, blocks_here, BLOCK, features), axis=2
    ).astype(bf16)
    copies = jnp.broadcast_to(pooled_here, (peers, *pooled_here.shape))
    everyone = lax.all_to_all(copies, "seq", split_axis=0, concat_axis=0, tiled=True)
    pooled = jnp.transpose(everyone, (1, 0, 2, 3)).reshape(2, peers * blocks_here, features)
    chosen = jnp.repeat(block_choice, BLOCK, axis=0)
    gates = branch_gates.reshape(tokens, -1)
    route_w = ROUTE_SCALE * route_scores / jnp.sum(route_scores, axis=1, keepdims=True)
    w_up = jnp.transpose(w_gate_up[0], (1, 2, 0))
    gain = norm_gain[None, :]
    att, slot, weight, *xs = attention(
        meta, chosen, expert_ids.T, route_w.T, gates, queries, pieces, pooled, PARTS, peers
    )

    def exchanged(x, n):
        return lax.all_to_all(
            x.reshape(peers, n, features), "seq", split_axis=0, concat_axis=0, tiled=True
        ).reshape(peers * n, features)

    to_right = [(i, (i + 1) % ring) for i in range(ring)]
    to_left = [(i, (i - 1) % ring) for i in range(ring)]
    send_right = lambda x: lax.ppermute(x, "exp", to_right)
    send_left = lambda x: lax.ppermute(x, "exp", to_left)
    order = [0, -1, -2, -3, 1, 2, 3, 4]
    places = jnp.stack([(me + k) % ring for k in order]).astype(jnp.int32)
    middle = half // 2
    summed = []
    for x, n in zip(xs, PARTS):
        whole = project(gain, exchanged(x, n), w_up, ring)
        summed.append(
            lax.psum_scatter(whole.reshape(-1, peers * n), "exp", scatter_dimension=0, tiled=True)
        )
    mixed = att
    base = 0
    for c, n in enumerate(PARTS):
        act = activate(summed[c], half)
        rights, lefts = [act], [act]
        for _ in range(3):
            rights.append(send_right(rights[-1]))
            lefts.append(send_left(lefts[-1]))
        top, bottom = send_right(rights[-1][:middle]), send_left(lefts[-1][middle:])
        result = down(places, [*rights, *lefts[1:], top, bottom], w_down[0])
        back = exchanged(result, n)
        last = c == len(PARTS) - 1
        mixed = combine(slot, weight, mixed, back, base, n, bf16 if last else f32)
        base += n
    return mixed


def solution(mesh):
    placed = (
        P("seq", "exp"),
        P("seq", "exp"),
        P("seq", "exp"),
        P("seq", None, "exp"),
        P("seq", None),
        P("exp"),
        P("seq", None),
        P("seq", None),
        P("seq", "exp", None, None),
        P("seq", None, "exp"),
    )

    return jax.shard_map(
        local, mesh=mesh, in_specs=placed, out_specs=P("seq", "exp"), check_vma=False
    )
```

```python
import functools

import jax
import jax.numpy as jnp
from jax import lax
from jax.experimental import pallas as pl
from jax.experimental.pallas import tpu as pltpu
from jax.sharding import PartitionSpec as P


HD = 128
D = 7168
BLOCK = 64
EPSILON = 1e-06
ROUTE_SCALE = 2.5
MASKED = -1e30
SUB = 8
PARTS = (16, 24)

f32 = jnp.float32
bf16 = jnp.bfloat16


def mm(a, b, ca, cb):
    return lax.dot_general(a, b, (((ca,), (cb,)), ((), ())), preferred_element_type=f32)


def tables_kernel(
    meta, chosen, ids, route_w, bias, cbias, onehot, slot_out, weight_out, *, pieces, slots
):
    experts, tokens = slot_out.shape
    row = meta[0]
    blocks_here = tokens // BLOCK
    q_in = lax.broadcasted_iota(jnp.int32, (tokens, tokens), 0)
    k_in = lax.broadcasted_iota(jnp.int32, (tokens, tokens), 1)
    gap = q_in // BLOCK - k_in // BLOCK
    for p in range(pieces):
        delta = meta[1 + p]
        offset = gap + blocks_here * delta
        hit = offset == chosen[:, 0:1]
        for j in range(1, chosen.shape[1]):
            hit = hit | (offset == chosen[:, j : j + 1])
        ok = hit & (row >= delta)
        if p == 0:
            ok = ok & (k_in <= q_in)
        bias[:, p * tokens : (p + 1) * tokens] = jnp.where(ok, 0.0, MASKED)
    cq = lax.broadcasted_iota(jnp.int32, cbias.shape, 0) // BLOCK + row * blocks_here
    cb = lax.broadcasted_iota(jnp.int32, cbias.shape, 1)
    cbias[...] = jnp.where(cb < cq, 0.0, MASKED)
    expert = lax.broadcasted_iota(jnp.int32, (experts, tokens), 0)
    named = jnp.zeros((experts, tokens), f32)
    weight = jnp.zeros((experts, tokens), f32)
    for k in range(ids.shape[0]):
        same = expert == ids[k : k + 1, :]
        named = jnp.where(same, 1.0, named)
        weight = jnp.where(same, route_w[k : k + 1, :], weight)
    before = jnp.where(q_in < k_in, 1.0, 0.0).astype(bf16)
    count = mm(named.astype(bf16), before, 1, 0)
    slot = jnp.where(named > 0.5, count, -1.0)
    slot_out[...] = slot
    weight_out[...] = weight
    base = 0
    for n in slots:
        at = (lax.broadcasted_iota(jnp.int32, (experts, n, tokens), 1) + base).astype(f32)
        hot = jnp.where(slot[:, None, :] == at, 1.0, 0.0)
        onehot[base * experts : (base + n) * experts, :] = hot.reshape(
            experts * n, tokens
        ).astype(bf16)
        base += n


def tables(meta, chosen, ids, route_w, pieces, all_blocks, slots, experts):
    tokens = chosen.shape[0]

    def whole(a):
        return pl.BlockSpec(a.shape, lambda i, m: (0,) * len(a.shape))

    outs = [
        jax.ShapeDtypeStruct((tokens, pieces * tokens), f32),
        jax.ShapeDtypeStruct((tokens, all_blocks), f32),
        jax.ShapeDtypeStruct((experts * sum(slots), tokens), bf16),
        jax.ShapeDtypeStruct((experts, tokens), f32),
        jax.ShapeDtypeStruct((experts, tokens), f32),
    ]
    return pl.pallas_call(
        functools.partial(tables_kernel, pieces=pieces, slots=slots),
        name="tables",
        grid_spec=pltpu.PrefetchScalarGridSpec(
            num_scalar_prefetch=1,
            grid=(1,),
            in_specs=[whole(a) for a in (chosen, ids, route_w)],
            out_specs=[whole(a) for a in outs],
        ),
        out_shape=outs,
    )(meta, chosen, ids, route_w)


def attention_kernel(bias, cbias, onehot, gates, q, *refs, pieces, slots, experts, heads):
    kv = refs[:pieces]
    pooled, att_out, *x_outs = refs[pieces:]
    h = pl.program_id(0)
    scale = HD ** (-0.5)
    qh = q[...]
    keys = jnp.concatenate([piece[0] for piece in kv], axis=0)
    s = mm(qh, keys, 1, 1) * scale + bias[...]
    top = jnp.max(s, axis=1, keepdims=True)
    w = jnp.exp(s - top)
    total = jnp.sum(w, axis=1, keepdims=True)
    values = jnp.concatenate([piece[1] for piece in kv], axis=0)
    fine = mm(w.astype(bf16), values, 1, 0)
    cs = mm(qh, pooled[0], 1, 1) * scale + cbias[...]
    ctop = jnp.max(cs, axis=1, keepdims=True)
    ctop = jnp.where(ctop > 0.5 * MASKED, ctop, 0.0)
    cw = jnp.exp(cs - ctop)
    ctotal = jnp.maximum(jnp.sum(cw, axis=1, keepdims=True), 1.0)
    coarse = mm(cw.astype(bf16), pooled[1], 1, 0)
    lane = lax.broadcasted_iota(jnp.int32, gates.shape, 1)
    gate_c = jnp.sum(jnp.where(lane == h, gates[...], 0.0), axis=1, keepdims=True)
    gate_f = jnp.sum(jnp.where(lane == h + heads, gates[...], 0.0), axis=1, keepdims=True)
    att = (gate_c / ctotal * coarse + gate_f / total * fine).astype(bf16)
    att_out[...] = att
    base = 0
    for x_out, n in zip(x_outs, slots):
        rows = slice(base * experts, (base + n) * experts)
        x_out[...] = mm(onehot[rows, :], att, 1, 0).astype(bf16)
        base += n


def attention(bias, cbias, onehot, gates, q, kv, pooled, slots, experts):
    features = q.shape[1]
    heads = features // HD

    def whole(a):
        return pl.BlockSpec(a.shape, lambda h: (0,) * len(a.shape))

    def per_head(a):
        zeros = (0,) * (len(a.shape) - 1)
        return pl.BlockSpec((*a.shape[:-1], HD), lambda h: (*zeros, h))

    small = [bias, cbias, onehot, gates]
    wide = [q, *kv, pooled]
    outs = [
        jax.ShapeDtypeStruct(q.shape, bf16),
        *[jax.ShapeDtypeStruct((experts * n, features), bf16) for n in slots],
    ]
    return pl.pallas_call(
        functools.partial(
            attention_kernel, pieces=len(kv), slots=slots, experts=experts, heads=heads
        ),
        name="attend",
        grid=(heads,),
        in_specs=[whole(a) for a in small] + [per_head(a) for a in wide],
        out_specs=[per_head(a) for a in outs],
        out_shape=outs,
    )(*small, *wide)


def project_kernel(gain, x, gate_w, up_w, out, scaled, square):
    half = gate_w.shape[1] // out.shape[0]

    @pl.when(pl.program_id(0) == 0)
    def _():
        wide = x[...].astype(f32)
        scaled[...] = (wide * gain[...]).astype(bf16)
        square[...] = mm(
            jnp.ones((SUB, x.shape[1]), bf16), (wide * wide).astype(bf16), 1, 1
        ).astype(bf16)

    gate = mm(gate_w[0], scaled[...], 1, 1).astype(bf16)
    up = mm(up_w[0], scaled[...], 1, 1).astype(bf16)
    for k in range(out.shape[0]):
        out[k, :half, :] = gate[k * half : (k + 1) * half]
        out[k, half : 2 * half, :] = up[k * half : (k + 1) * half]
        out[k, 2 * half :, :] = square[...]


def project(gain, x, w, shards, pair=2):
    _, hidden, features = w.shape
    half = hidden // shards
    rows = x.shape[0]
    return pl.pallas_call(
        project_kernel,
        name="project",
        grid=(shards // pair,),
        in_specs=[
            pl.BlockSpec((1, features), lambda z: (0, 0)),
            pl.BlockSpec((rows, features), lambda z: (0, 0)),
            pl.BlockSpec((1, pair * half, features), lambda z: (0, z, 0)),
            pl.BlockSpec((1, pair * half, features), lambda z: (1, z, 0)),
        ],
        out_specs=pl.BlockSpec((pair, 2 * half + SUB, rows), lambda z: (z, 0, 0)),
        out_shape=jax.ShapeDtypeStruct((shards, 2 * half + SUB, rows), bf16),
        scratch_shapes=[pltpu.VMEM((rows, features), bf16), pltpu.VMEM((SUB, rows), bf16)],
    )(gain, x, w, w)


def activate_kernel(summed, out):
    half = out.shape[0]
    r = lax.rsqrt(summed[2 * half : 2 * half + 1, :].astype(f32) / D + EPSILON)
    gate = summed[:half, :].astype(f32) * r
    up = summed[half : 2 * half, :].astype(f32) * r
    out[...] = (gate / (1.0 + jnp.exp(-gate)) * up).astype(bf16)


def activate(summed, half):
    rows = summed.shape[1]
    return pl.pallas_call(
        activate_kernel,
        name="activate",
        grid=(1,),
        in_specs=[pl.BlockSpec(summed.shape, lambda i: (0, 0))],
        out_specs=pl.BlockSpec((half, rows), lambda i: (0, 0)),
        out_shape=jax.ShapeDtypeStruct((half, rows), bf16),
    )(summed)


def down_kernel(places, *refs):
    acts, (top, bottom, w, out, joined) = refs[:-5], refs[-5:]
    half = acts[0].shape[0]

    def put(k, offset, a):
        start = pl.multiple_of(places[k] * half + offset, 32)
        joined[pl.ds(start, a.shape[0]), :] = a[...]

    for k, a in enumerate(acts):
        put(k, 0, a)
    put(len(acts), 0, top)
    put(len(acts), top.shape[0], bottom)
    out[...] = mm(joined[...], w[...], 0, 0).astype(bf16)


def down(places, acts, w, tile=256):
    rows = acts[0].shape[1]
    hidden, features = w.shape
    return pl.pallas_call(
        down_kernel,
        name="down",
        grid_spec=pltpu.PrefetchScalarGridSpec(
            num_scalar_prefetch=1,
            grid=(rows // tile,),
            in_specs=[pl.BlockSpec((a.shape[0], tile), lambda i, a: (0, i)) for a in acts]
            + [pl.BlockSpec((hidden, features), lambda i, a: (0, 0))],
            out_specs=pl.BlockSpec((tile, features), lambda i, a: (i, 0)),
            scratch_shapes=[pltpu.VMEM((hidden, tile), bf16)],
        ),
        out_shape=jax.ShapeDtypeStruct((rows, features), bf16),
    )(places, *acts, w)


def combine_kernel(slot, weight, x, back, out, *, base, slots):
    experts, tokens = slot.shape
    at = (lax.broadcasted_iota(jnp.int32, (experts, slots, tokens), 1) + base).astype(f32)
    hot = jnp.where(slot[...][:, None, :] == at, weight[...][:, None, :], 0.0)
    mix = hot.reshape(experts * slots, tokens).astype(bf16)
    out[...] = (x[...].astype(f32) + mm(mix, back[...], 0, 0)).astype(out.dtype)


def combine(slot, weight, x, back, base, slots, dtype):
    whole = lambda a: pl.BlockSpec(a.shape, lambda i: (0,) * a.ndim)
    return pl.pallas_call(
        functools.partial(combine_kernel, base=base, slots=slots),
        name="combine",
        grid=(1,),
        in_specs=[whole(slot), whole(weight), whole(x), whole(back)],
        out_specs=whole(x),
        out_shape=jax.ShapeDtypeStruct(x.shape, dtype),
    )(slot, weight, x, back)


def local(
    queries,
    keys,
    values,
    branch_gates,
    block_choice,
    norm_gain,
    expert_ids,
    route_scores,
    w_gate_up,
    w_down,
):
    tokens, features = queries.shape
    blocks_here = tokens // BLOCK
    row = lax.axis_index("seq")
    peers = lax.axis_size("seq")
    me = lax.axis_index("exp")
    ring = lax.axis_size("exp")
    hidden = w_down.shape[1]
    half = hidden // ring

    kv = jnp.stack([keys, values])

    across = 2 * 4
    chip = (row % across) // 2
    odd = row % 2

    def shifted(x, by):
        pairs = [(i, i - i % across + (i + 2 * by) % across) for i in range(peers)]
        return lax.ppermute(x, "seq", pairs)

    def swapped(x):
        return lax.ppermute(x, "seq", [(i, i ^ 1) for i in range(peers)])

    above = lax.ppermute(kv, "seq", [(i, i + across) for i in range(peers - across)])
    far = [shifted(jnp.where(chip >= 4 - by, above, kv), by) for by in (1, 2, 3)]
    beside = swapped(jnp.where(odd == 1, above, kv))
    pieces = [kv, *far, beside, *[swapped(x) for x in far]]
    meta = jnp.stack(
        [row]
        + [jnp.int32(d) for d in (0, 2, 4, 6)]
        + [jnp.where(odd == 1, 1, 7)]
        + [d + 2 * odd for d in (1, 3, 5)]
    ).astype(jnp.int32)
    pooled_here = jnp.mean(
        kv.astype(f32).reshape(2, blocks_here, BLOCK, features), axis=2
    ).astype(bf16)
    copies = jnp.broadcast_to(pooled_here, (peers, *pooled_here.shape))
    everyone = lax.all_to_all(copies, "seq", split_axis=0, concat_axis=0, tiled=True)
    pooled = jnp.transpose(everyone, (1, 0, 2, 3)).reshape(2, peers * blocks_here, features)
    chosen = jnp.repeat(block_choice, BLOCK, axis=0)
    gates = branch_gates.reshape(tokens, -1)
    route_w = ROUTE_SCALE * route_scores / jnp.sum(route_scores, axis=1, keepdims=True)
    w_up = jnp.transpose(w_gate_up[0], (1, 2, 0))
    gain = norm_gain[None, :]
    bias, cbias, onehot, slot, weight = tables(
        meta, chosen, expert_ids.T, route_w.T, len(pieces), pooled.shape[1], PARTS, peers
    )
    att, *xs = attention(bias, cbias, onehot, gates, queries, pieces, pooled, PARTS, peers)

    def exchanged(x, n):
        return lax.all_to_all(
            x.reshape(peers, n, features), "seq", split_axis=0, concat_axis=0, tiled=True
        ).reshape(peers * n, features)

    to_right = [(i, (i + 1) % ring) for i in range(ring)]
    to_left = [(i, (i - 1) % ring) for i in range(ring)]
    send_right = lambda x: lax.ppermute(x, "exp", to_right)
    send_left = lambda x: lax.ppermute(x, "exp", to_left)
    order = [0, -1, -2, -3, 1, 2, 3, 4]
    places = jnp.stack([(me + k) % ring for k in order]).astype(jnp.int32)
    middle = half // 2
    summed = []
    for x, n in zip(xs, PARTS):
        whole = project(gain, exchanged(x, n), w_up, ring)
        summed.append(
            lax.psum_scatter(whole.reshape(-1, peers * n), "exp", scatter_dimension=0, tiled=True)
        )
    mixed = att
    base = 0
    for c, n in enumerate(PARTS):
        act = activate(summed[c], half)
        rights, lefts = [act], [act]
        for _ in range(3):
            rights.append(send_right(rights[-1]))
            lefts.append(send_left(lefts[-1]))
        top, bottom = send_right(rights[-1][:middle]), send_left(lefts[-1][middle:])
        result = down(places, [*rights, *lefts[1:], top, bottom], w_down[0])
        back = exchanged(result, n)
        last = c == len(PARTS) - 1
        mixed = combine(slot, weight, mixed, back, base, n, bf16 if last else f32)
        base += n
    return mixed


def solution(mesh):
    placed = (
        P("seq", "exp"),
        P("seq", "exp"),
        P("seq", "exp"),
        P("seq", None, "exp"),
        P("seq", None),
        P("exp"),
        P("seq", None),
        P("seq", None),
        P("seq", "exp", None, None),
        P("seq", None, "exp"),
    )

    return jax.shard_map(
        local, mesh=mesh, in_specs=placed, out_specs=P("seq", "exp"), check_vma=False
    )
```

```python
import functools

import jax
import jax.numpy as jnp
from jax import lax
from jax.experimental import pallas as pl
from jax.experimental.pallas import tpu as pltpu
from jax.sharding import PartitionSpec as P


HD = 128
D = 7168
BLOCK = 64
EPSILON = 1e-06
ROUTE_SCALE = 2.5
MASKED = -1e30
SUB = 8
PARTS = (16, 24)

f32 = jnp.float32
bf16 = jnp.bfloat16


def mm(a, b, ca, cb):
    return lax.dot_general(a, b, (((ca,), (cb,)), ((), ())), preferred_element_type=f32)


def tables_kernel(
    meta, chosen, ids, bias, cbias, onehot, slot_out, *, pieces, slots
):
    experts, tokens = slot_out.shape
    row = meta[0]
    blocks_here = tokens // BLOCK
    q_in = lax.broadcasted_iota(jnp.int32, (tokens, tokens), 0)
    k_in = lax.broadcasted_iota(jnp.int32, (tokens, tokens), 1)
    gap = q_in // BLOCK - k_in // BLOCK
    for p in range(pieces):
        delta = meta[1 + p]
        offset = gap + blocks_here * delta
        hit = offset == chosen[:, 0:1]
        for j in range(1, chosen.shape[1]):
            hit = hit | (offset == chosen[:, j : j + 1])
        ok = hit & (row >= delta)
        if p == 0:
            ok = ok & (k_in <= q_in)
        bias[:, p * tokens : (p + 1) * tokens] = jnp.where(ok, 0.0, MASKED)
    cq = lax.broadcasted_iota(jnp.int32, cbias.shape, 0) // BLOCK + row * blocks_here
    cb = lax.broadcasted_iota(jnp.int32, cbias.shape, 1)
    cbias[...] = jnp.where(cb < cq, 0.0, MASKED)
    expert = lax.broadcasted_iota(jnp.int32, (experts, tokens), 0)
    named = jnp.zeros((experts, tokens), f32)
    for k in range(ids.shape[0]):
        named = jnp.where(expert == ids[k : k + 1, :], 1.0, named)
    before = jnp.where(q_in < k_in, 1.0, 0.0).astype(bf16)
    count = mm(named.astype(bf16), before, 1, 0)
    slot = jnp.where(named > 0.5, count, -1.0)
    slot_out[...] = slot
    base = 0
    for n in slots:
        at = (lax.broadcasted_iota(jnp.int32, (experts, n, tokens), 1) + base).astype(f32)
        hot = jnp.where(slot[:, None, :] == at, 1.0, 0.0)
        onehot[base * experts : (base + n) * experts, :] = hot.reshape(
            experts * n, tokens
        ).astype(bf16)
        base += n


def tables(meta, chosen, ids, pieces, all_blocks, slots, experts):
    tokens = chosen.shape[0]

    def whole(a):
        return pl.BlockSpec(a.shape, lambda i, m: (0,) * len(a.shape))

    outs = [
        jax.ShapeDtypeStruct((tokens, pieces * tokens), f32),
        jax.ShapeDtypeStruct((tokens, all_blocks), f32),
        jax.ShapeDtypeStruct((experts * sum(slots), tokens), bf16),
        jax.ShapeDtypeStruct((experts, tokens), f32),
    ]
    return pl.pallas_call(
        functools.partial(tables_kernel, pieces=pieces, slots=slots),
        name="tables",
        grid_spec=pltpu.PrefetchScalarGridSpec(
            num_scalar_prefetch=1,
            grid=(1,),
            in_specs=[whole(chosen), whole(ids)],
            out_specs=[whole(a) for a in outs],
        ),
        out_shape=outs,
    )(meta, chosen, ids)


def attention_kernel(bias, cbias, onehot, gates, q, *refs, pieces, slots, experts, heads):
    kv = refs[:pieces]
    pooled, att_out, *x_outs = refs[pieces:]
    h = pl.program_id(0)
    scale = HD ** (-0.5)
    qh = q[...]
    keys = jnp.concatenate([piece[0] for piece in kv], axis=0)
    s = mm(qh, keys, 1, 1) * scale + bias[...]
    top = jnp.max(s, axis=1, keepdims=True)
    w = jnp.exp(s - top)
    total = jnp.sum(w, axis=1, keepdims=True)
    values = jnp.concatenate([piece[1] for piece in kv], axis=0)
    fine = mm(w.astype(bf16), values, 1, 0)
    cs = mm(qh, pooled[0], 1, 1) * scale + cbias[...]
    ctop = jnp.max(cs, axis=1, keepdims=True)
    ctop = jnp.where(ctop > 0.5 * MASKED, ctop, 0.0)
    cw = jnp.exp(cs - ctop)
    ctotal = jnp.maximum(jnp.sum(cw, axis=1, keepdims=True), 1.0)
    coarse = mm(cw.astype(bf16), pooled[1], 1, 0)
    lane = lax.broadcasted_iota(jnp.int32, gates.shape, 1)
    gate_c = jnp.sum(jnp.where(lane == h, gates[...], 0.0), axis=1, keepdims=True)
    gate_f = jnp.sum(jnp.where(lane == h + heads, gates[...], 0.0), axis=1, keepdims=True)
    att = (gate_c / ctotal * coarse + gate_f / total * fine).astype(bf16)
    att_out[...] = att
    base = 0
    for x_out, n in zip(x_outs, slots):
        rows = slice(base * experts, (base + n) * experts)
        x_out[...] = mm(onehot[rows, :], att, 1, 0).astype(bf16)
        base += n


def attention(bias, cbias, onehot, gates, q, kv, pooled, slots, experts):
    features = q.shape[1]
    heads = features // HD

    def whole(a):
        return pl.BlockSpec(a.shape, lambda h: (0,) * len(a.shape))

    def per_head(a):
        zeros = (0,) * (len(a.shape) - 1)
        return pl.BlockSpec((*a.shape[:-1], HD), lambda h: (*zeros, h))

    small = [bias, cbias, onehot, gates]
    wide = [q, *kv, pooled]
    outs = [
        jax.ShapeDtypeStruct(q.shape, bf16),
        *[jax.ShapeDtypeStruct((experts * n, features), bf16) for n in slots],
    ]
    return pl.pallas_call(
        functools.partial(
            attention_kernel, pieces=len(kv), slots=slots, experts=experts, heads=heads
        ),
        name="attend",
        grid=(heads,),
        in_specs=[whole(a) for a in small] + [per_head(a) for a in wide],
        out_specs=[per_head(a) for a in outs],
        out_shape=outs,
    )(*small, *wide)


def project_kernel(gain, x, gate_w, up_w, out, scaled, square):
    half = gate_w.shape[1] // out.shape[0]

    @pl.when(pl.program_id(0) == 0)
    def _():
        wide = x[...].astype(f32)
        scaled[...] = (wide * gain[...]).astype(bf16)
        square[...] = mm(
            jnp.ones((SUB, x.shape[1]), bf16), (wide * wide).astype(bf16), 1, 1
        ).astype(bf16)

    gate = mm(gate_w[0], scaled[...], 1, 1).astype(bf16)
    up = mm(up_w[0], scaled[...], 1, 1).astype(bf16)
    for k in range(out.shape[0]):
        out[k, :half, :] = gate[k * half : (k + 1) * half]
        out[k, half : 2 * half, :] = up[k * half : (k + 1) * half]
        out[k, 2 * half :, :] = square[...]


def project(gain, x, w, shards, pair=2):
    _, hidden, features = w.shape
    half = hidden // shards
    rows = x.shape[0]
    return pl.pallas_call(
        project_kernel,
        name="project",
        grid=(shards // pair,),
        in_specs=[
            pl.BlockSpec((1, features), lambda z: (0, 0)),
            pl.BlockSpec((rows, features), lambda z: (0, 0)),
            pl.BlockSpec((1, pair * half, features), lambda z: (0, z, 0)),
            pl.BlockSpec((1, pair * half, features), lambda z: (1, z, 0)),
        ],
        out_specs=pl.BlockSpec((pair, 2 * half + SUB, rows), lambda z: (z, 0, 0)),
        out_shape=jax.ShapeDtypeStruct((shards, 2 * half + SUB, rows), bf16),
        scratch_shapes=[pltpu.VMEM((rows, features), bf16), pltpu.VMEM((SUB, rows), bf16)],
    )(gain, x, w, w)


def activate_kernel(summed, out):
    half = out.shape[0]
    r = lax.rsqrt(summed[2 * half : 2 * half + 1, :].astype(f32) / D + EPSILON)
    gate = summed[:half, :].astype(f32) * r
    up = summed[half : 2 * half, :].astype(f32) * r
    out[...] = (gate / (1.0 + jnp.exp(-gate)) * up).astype(bf16)


def activate(summed, half):
    rows = summed.shape[1]
    return pl.pallas_call(
        activate_kernel,
        name="activate",
        grid=(1,),
        in_specs=[pl.BlockSpec(summed.shape, lambda i: (0, 0))],
        out_specs=pl.BlockSpec((half, rows), lambda i: (0, 0)),
        out_shape=jax.ShapeDtypeStruct((half, rows), bf16),
    )(summed)


def down_kernel(places, *refs):
    acts, (top, bottom, w, out, joined) = refs[:-5], refs[-5:]
    half = acts[0].shape[0]

    def put(k, offset, a):
        start = pl.multiple_of(places[k] * half + offset, 32)
        joined[pl.ds(start, a.shape[0]), :] = a[...]

    for k, a in enumerate(acts):
        put(k, 0, a)
    put(len(acts), 0, top)
    put(len(acts), top.shape[0], bottom)
    out[...] = mm(joined[...], w[...], 0, 0).astype(bf16)


def down(places, acts, w, tile=256):
    rows = acts[0].shape[1]
    hidden, features = w.shape
    return pl.pallas_call(
        down_kernel,
        name="down",
        grid_spec=pltpu.PrefetchScalarGridSpec(
            num_scalar_prefetch=1,
            grid=(rows // tile,),
            in_specs=[pl.BlockSpec((a.shape[0], tile), lambda i, a: (0, i)) for a in acts]
            + [pl.BlockSpec((hidden, features), lambda i, a: (0, 0))],
            out_specs=pl.BlockSpec((tile, features), lambda i, a: (i, 0)),
            scratch_shapes=[pltpu.VMEM((hidden, tile), bf16)],
        ),
        out_shape=jax.ShapeDtypeStruct((rows, features), bf16),
    )(places, *acts, w)


def combine_kernel(slot, ids, scores, x, back, out, *, base, slots):
    experts, tokens = slot.shape
    route_w = ROUTE_SCALE * scores[...] / jnp.sum(scores[...], axis=0, keepdims=True)
    expert = lax.broadcasted_iota(jnp.int32, (experts, tokens), 0)
    weight = jnp.zeros((experts, tokens), f32)
    for k in range(ids.shape[0]):
        weight = jnp.where(expert == ids[k : k + 1, :], route_w[k : k + 1, :], weight)
    at = (lax.broadcasted_iota(jnp.int32, (experts, slots, tokens), 1) + base).astype(f32)
    hot = jnp.where(slot[...][:, None, :] == at, weight[:, None, :], 0.0)
    mix = hot.reshape(experts * slots, tokens).astype(bf16)
    out[...] = (x[...].astype(f32) + mm(mix, back[...], 0, 0)).astype(out.dtype)


def combine(slot, ids, scores, x, back, base, slots, dtype):
    whole = lambda a: pl.BlockSpec(a.shape, lambda i: (0,) * a.ndim)
    return pl.pallas_call(
        functools.partial(combine_kernel, base=base, slots=slots),
        name="combine",
        grid=(1,),
        in_specs=[whole(a) for a in (slot, ids, scores, x, back)],
        out_specs=whole(x),
        out_shape=jax.ShapeDtypeStruct(x.shape, dtype),
    )(slot, ids, scores, x, back)


def local(
    queries,
    keys,
    values,
    branch_gates,
    block_choice,
    norm_gain,
    expert_ids,
    route_scores,
    w_gate_up,
    w_down,
):
    tokens, features = queries.shape
    blocks_here = tokens // BLOCK
    row = lax.axis_index("seq")
    peers = lax.axis_size("seq")
    me = lax.axis_index("exp")
    ring = lax.axis_size("exp")
    hidden = w_down.shape[1]
    half = hidden // ring

    kv = jnp.stack([keys, values])

    across = 2 * 4
    chip = (row % across) // 2
    odd = row % 2

    def shifted(x, by):
        pairs = [(i, i - i % across + (i + 2 * by) % across) for i in range(peers)]
        return lax.ppermute(x, "seq", pairs)

    def swapped(x):
        return lax.ppermute(x, "seq", [(i, i ^ 1) for i in range(peers)])

    above = lax.ppermute(kv, "seq", [(i, i + across) for i in range(peers - across)])
    far = [shifted(jnp.where(chip >= 4 - by, above, kv), by) for by in (1, 2, 3)]
    beside = swapped(jnp.where(odd == 1, above, kv))
    pieces = [kv, *far, beside, *[swapped(x) for x in far]]
    meta = jnp.stack(
        [row]
        + [jnp.int32(d) for d in (0, 2, 4, 6)]
        + [jnp.where(odd == 1, 1, 7)]
        + [d + 2 * odd for d in (1, 3, 5)]
    ).astype(jnp.int32)
    pooled_here = jnp.mean(
        kv.astype(f32).reshape(2, blocks_here, BLOCK, features), axis=2
    ).astype(bf16)
    copies = jnp.broadcast_to(pooled_here, (peers, *pooled_here.shape))
    everyone = lax.all_to_all(copies, "seq", split_axis=0, concat_axis=0, tiled=True)
    pooled = jnp.transpose(everyone, (1, 0, 2, 3)).reshape(2, peers * blocks_here, features)
    chosen = jnp.repeat(block_choice, BLOCK, axis=0)
    gates = branch_gates.reshape(tokens, -1)
    w_up = jnp.transpose(w_gate_up[0], (1, 2, 0))
    gain = norm_gain[None, :]
    bias, cbias, onehot, slot = tables(
        meta, chosen, expert_ids.T, len(pieces), pooled.shape[1], PARTS, peers
    )
    att, *xs = attention(bias, cbias, onehot, gates, queries, pieces, pooled, PARTS, peers)

    def exchanged(x, n):
        return lax.all_to_all(
            x.reshape(peers, n, features), "seq", split_axis=0, concat_axis=0, tiled=True
        ).reshape(peers * n, features)

    to_right = [(i, (i + 1) % ring) for i in range(ring)]
    to_left = [(i, (i - 1) % ring) for i in range(ring)]
    send_right = lambda x: lax.ppermute(x, "exp", to_right)
    send_left = lambda x: lax.ppermute(x, "exp", to_left)
    order = [0, -1, -2, -3, 1, 2, 3, 4]
    places = jnp.stack([(me + k) % ring for k in order]).astype(jnp.int32)
    middle = half // 2
    summed = []
    for x, n in zip(xs, PARTS):
        whole = project(gain, exchanged(x, n), w_up, ring)
        summed.append(
            lax.psum_scatter(whole.reshape(-1, peers * n), "exp", scatter_dimension=0, tiled=True)
        )
    mixed = att
    base = 0
    for c, n in enumerate(PARTS):
        act = activate(summed[c], half)
        rights, lefts = [act], [act]
        for _ in range(3):
            rights.append(send_right(rights[-1]))
            lefts.append(send_left(lefts[-1]))
        top, bottom = send_right(rights[-1][:middle]), send_left(lefts[-1][middle:])
        result = down(places, [*rights, *lefts[1:], top, bottom], w_down[0])
        back = exchanged(result, n)
        last = c == len(PARTS) - 1
        mixed = combine(
            slot, expert_ids.T, route_scores.T, mixed, back, base, n, bf16 if last else f32
        )
        base += n
    return mixed


def solution(mesh):
    placed = (
        P("seq", "exp"),
        P("seq", "exp"),
        P("seq", "exp"),
        P("seq", None, "exp"),
        P("seq", None),
        P("exp"),
        P("seq", None),
        P("seq", None),
        P("seq", "exp", None, None),
        P("seq", None, "exp"),
    )

    return jax.shard_map(
        local, mesh=mesh, in_specs=placed, out_specs=P("seq", "exp"), check_vma=False
    )
```

```python
import functools

import jax
import jax.numpy as jnp
from jax import lax
from jax.experimental import pallas as pl
from jax.experimental.pallas import tpu as pltpu
from jax.sharding import PartitionSpec as P


HD = 128
D = 7168
BLOCK = 64
EPSILON = 1e-06
ROUTE_SCALE = 2.5
MASKED = -1e30
SUB = 8
PARTS = (16, 24)

f32 = jnp.float32
bf16 = jnp.bfloat16


def mm(a, b, ca, cb):
    return lax.dot_general(a, b, (((ca,), (cb,)), ((), ())), preferred_element_type=f32)


def tables_kernel(
    meta, chosen, ids, bias, cbias, onehot, slot_out, *, pieces, slots
):
    experts, tokens = slot_out.shape
    row = meta[0]
    blocks_here = tokens // BLOCK
    q_in = lax.broadcasted_iota(jnp.int32, (tokens, tokens), 0)
    k_in = lax.broadcasted_iota(jnp.int32, (tokens, tokens), 1)
    gap = q_in // BLOCK - k_in // BLOCK
    for p in range(pieces):
        delta = meta[1 + p]
        offset = gap + blocks_here * delta
        hit = offset == chosen[:, 0:1]
        for j in range(1, chosen.shape[1]):
            hit = hit | (offset == chosen[:, j : j + 1])
        ok = hit & (row >= delta)
        if p == 0:
            ok = ok & (k_in <= q_in)
        bias[:, p * tokens : (p + 1) * tokens] = jnp.where(ok, 0.0, MASKED)
    cq = lax.broadcasted_iota(jnp.int32, cbias.shape, 0) // BLOCK + row * blocks_here
    cb = lax.broadcasted_iota(jnp.int32, cbias.shape, 1)
    cbias[...] = jnp.where(cb < cq, 0.0, MASKED)
    expert = lax.broadcasted_iota(jnp.int32, (experts, tokens), 0)
    named = jnp.zeros((experts, tokens), f32)
    for k in range(ids.shape[0]):
        named = jnp.where(expert == ids[k : k + 1, :], 1.0, named)
    before = jnp.where(q_in < k_in, 1.0, 0.0).astype(bf16)
    count = mm(named.astype(bf16), before, 1, 0)
    slot = jnp.where(named > 0.5, count, -1.0)
    slot_out[...] = slot
    base = 0
    for n in slots:
        at = (lax.broadcasted_iota(jnp.int32, (experts, n, tokens), 1) + base).astype(f32)
        hot = jnp.where(slot[:, None, :] == at, 1.0, 0.0)
        onehot[base * experts : (base + n) * experts, :] = hot.reshape(
            experts * n, tokens
        ).astype(bf16)
        base += n


def tables(meta, chosen, ids, pieces, all_blocks, slots, experts):
    tokens = chosen.shape[0]

    def whole(a):
        return pl.BlockSpec(a.shape, lambda i, m: (0,) * len(a.shape))

    outs = [
        jax.ShapeDtypeStruct((tokens, pieces * tokens), f32),
        jax.ShapeDtypeStruct((tokens, all_blocks), f32),
        jax.ShapeDtypeStruct((experts * sum(slots), tokens), bf16),
        jax.ShapeDtypeStruct((experts, tokens), f32),
    ]
    return pl.pallas_call(
        functools.partial(tables_kernel, pieces=pieces, slots=slots),
        name="tables",
        grid_spec=pltpu.PrefetchScalarGridSpec(
            num_scalar_prefetch=1,
            grid=(1,),
            in_specs=[whole(chosen), whole(ids)],
            out_specs=[whole(a) for a in outs],
        ),
        out_shape=outs,
    )(meta, chosen, ids)


def attention_kernel(bias, cbias, onehot, gates, q, *refs, pieces, slots, experts, heads):
    kv = refs[:pieces]
    pooled, att_out, *x_outs = refs[pieces:]
    h = pl.program_id(0)
    scale = HD ** (-0.5)
    qh = q[...]
    keys = jnp.concatenate([piece[0] for piece in kv], axis=0)
    s = mm(qh, keys, 1, 1) * scale + bias[...]
    top = jnp.max(s, axis=1, keepdims=True)
    w = jnp.exp(s - top)
    total = jnp.sum(w, axis=1, keepdims=True)
    values = jnp.concatenate([piece[1] for piece in kv], axis=0)
    fine = mm(w.astype(bf16), values, 1, 0)
    cs = mm(qh, pooled[0], 1, 1) * scale + cbias[...]
    ctop = jnp.max(cs, axis=1, keepdims=True)
    ctop = jnp.where(ctop > 0.5 * MASKED, ctop, 0.0)
    cw = jnp.exp(cs - ctop)
    ctotal = jnp.maximum(jnp.sum(cw, axis=1, keepdims=True), 1.0)
    coarse = mm(cw.astype(bf16), pooled[1], 1, 0)
    lane = lax.broadcasted_iota(jnp.int32, gates.shape, 1)
    gate_c = jnp.sum(jnp.where(lane == h, gates[...], 0.0), axis=1, keepdims=True)
    gate_f = jnp.sum(jnp.where(lane == h + heads, gates[...], 0.0), axis=1, keepdims=True)
    att = (gate_c / ctotal * coarse + gate_f / total * fine).astype(bf16)
    att_out[...] = att
    base = 0
    for x_out, n in zip(x_outs, slots):
        rows = slice(base * experts, (base + n) * experts)
        x_out[...] = mm(onehot[rows, :], att, 1, 0).astype(bf16)
        base += n


def attention(bias, cbias, onehot, gates, q, kv, pooled, slots, experts):
    features = q.shape[1]
    heads = features // HD

    def whole(a):
        return pl.BlockSpec(a.shape, lambda h: (0,) * len(a.shape))

    def per_head(a):
        zeros = (0,) * (len(a.shape) - 1)
        return pl.BlockSpec((*a.shape[:-1], HD), lambda h: (*zeros, h))

    small = [bias, cbias, onehot, gates]
    wide = [q, *kv, pooled]
    outs = [
        jax.ShapeDtypeStruct(q.shape, bf16),
        *[jax.ShapeDtypeStruct((experts * n, features), bf16) for n in slots],
    ]
    return pl.pallas_call(
        functools.partial(
            attention_kernel, pieces=len(kv), slots=slots, experts=experts, heads=heads
        ),
        name="attend",
        grid=(heads,),
        in_specs=[whole(a) for a in small] + [per_head(a) for a in wide],
        out_specs=[per_head(a) for a in outs],
        out_shape=outs,
    )(*small, *wide)


def project_kernel(gain, x, gate_w, up_w, out, scaled, square):
    half = gate_w.shape[1] // out.shape[0]

    @pl.when(pl.program_id(0) == 0)
    def _():
        wide = x[...].astype(f32)
        scaled[...] = (wide * gain[...]).astype(bf16)
        square[...] = mm(
            jnp.ones((SUB, x.shape[1]), bf16), (wide * wide).astype(bf16), 1, 1
        ).astype(bf16)

    gate = mm(gate_w[0], scaled[...], 1, 1).astype(bf16)
    up = mm(up_w[0], scaled[...], 1, 1).astype(bf16)
    for k in range(out.shape[0]):
        out[k, :half, :] = gate[k * half : (k + 1) * half]
        out[k, half : 2 * half, :] = up[k * half : (k + 1) * half]
        out[k, 2 * half :, :] = square[...]


def project(gain, x, w, shards, pair=2):
    _, hidden, features = w.shape
    half = hidden // shards
    rows = x.shape[0]
    return pl.pallas_call(
        project_kernel,
        name="project",
        grid=(shards // pair,),
        in_specs=[
            pl.BlockSpec((1, features), lambda z: (0, 0)),
            pl.BlockSpec((rows, features), lambda z: (0, 0)),
            pl.BlockSpec((1, pair * half, features), lambda z: (0, z, 0)),
            pl.BlockSpec((1, pair * half, features), lambda z: (1, z, 0)),
        ],
        out_specs=pl.BlockSpec((pair, 2 * half + SUB, rows), lambda z: (z, 0, 0)),
        out_shape=jax.ShapeDtypeStruct((shards, 2 * half + SUB, rows), bf16),
        scratch_shapes=[pltpu.VMEM((rows, features), bf16), pltpu.VMEM((SUB, rows), bf16)],
    )(gain, x, w, w)


def activate_kernel(summed, out):
    half = out.shape[0]
    r = lax.rsqrt(summed[2 * half : 2 * half + 1, :].astype(f32) / D + EPSILON)
    gate = summed[:half, :].astype(f32) * r
    up = summed[half : 2 * half, :].astype(f32) * r
    out[...] = (gate / (1.0 + jnp.exp(-gate)) * up).astype(bf16)


def activate(summed, half):
    rows = summed.shape[1]
    return pl.pallas_call(
        activate_kernel,
        name="activate",
        grid=(1,),
        in_specs=[pl.BlockSpec(summed.shape, lambda i: (0, 0))],
        out_specs=pl.BlockSpec((half, rows), lambda i: (0, 0)),
        out_shape=jax.ShapeDtypeStruct((half, rows), bf16),
    )(summed)


def down_kernel(places, *refs):
    acts, (top, bottom, w, out, joined) = refs[:-5], refs[-5:]
    half = acts[0].shape[0]

    def put(k, offset, a):
        start = pl.multiple_of(places[k] * half + offset, 32)
        joined[pl.ds(start, a.shape[0]), :] = a[...]

    for k, a in enumerate(acts):
        put(k, 0, a)
    put(len(acts), 0, top)
    put(len(acts), top.shape[0], bottom)
    out[...] = mm(joined[...], w[...], 0, 0).astype(bf16)


def down(places, acts, w, tile=256):
    rows = acts[0].shape[1]
    hidden, features = w.shape
    return pl.pallas_call(
        down_kernel,
        name="down",
        grid_spec=pltpu.PrefetchScalarGridSpec(
            num_scalar_prefetch=1,
            grid=(rows // tile,),
            in_specs=[pl.BlockSpec((a.shape[0], tile), lambda i, a: (0, i)) for a in acts]
            + [pl.BlockSpec((hidden, features), lambda i, a: (0, 0))],
            out_specs=pl.BlockSpec((tile, features), lambda i, a: (i, 0)),
            scratch_shapes=[pltpu.VMEM((hidden, tile), bf16)],
        ),
        out_shape=jax.ShapeDtypeStruct((rows, features), bf16),
    )(places, *acts, w)


def down_some_kernel(places, *refs, which, start):
    *acts, w, out = refs[1:] if start else refs
    half = acts[0].shape[0]
    picked = [w[pl.ds(pl.multiple_of(places[k] * half, 64), half), :] for k in which]
    total = mm(
        jnp.concatenate([a[...] for a in acts], axis=0), jnp.concatenate(picked, axis=0), 0, 0
    )
    if start:
        total = total + refs[0][...]
    out[...] = total.astype(out.dtype)


def down_some(places, acts, w, which, start=None, tile=256):
    rows = acts[0].shape[1]
    hidden, features = w.shape
    product = pl.BlockSpec((tile, features), lambda i, a: (i, 0))
    before = [] if start is None else [start]
    return pl.pallas_call(
        functools.partial(down_some_kernel, which=which, start=bool(before)),
        name="down_some",
        grid_spec=pltpu.PrefetchScalarGridSpec(
            num_scalar_prefetch=1,
            grid=(rows // tile,),
            in_specs=[product] * len(before)
            + [pl.BlockSpec((a.shape[0], tile), lambda i, a: (0, i)) for a in acts]
            + [pl.BlockSpec((hidden, features), lambda i, a: (0, 0))],
            out_specs=product,
        ),
        out_shape=jax.ShapeDtypeStruct((rows, features), bf16 if before else f32),
    )(places, *before, *acts, w)


def combine_kernel(slot, ids, scores, x, back, out, *, base, slots):
    experts, tokens = slot.shape
    route_w = ROUTE_SCALE * scores[...] / jnp.sum(scores[...], axis=0, keepdims=True)
    expert = lax.broadcasted_iota(jnp.int32, (experts, tokens), 0)
    weight = jnp.zeros((experts, tokens), f32)
    for k in range(ids.shape[0]):
        weight = jnp.where(expert == ids[k : k + 1, :], route_w[k : k + 1, :], weight)
    at = (lax.broadcasted_iota(jnp.int32, (experts, slots, tokens), 1) + base).astype(f32)
    hot = jnp.where(slot[...][:, None, :] == at, weight[:, None, :], 0.0)
    mix = hot.reshape(experts * slots, tokens).astype(bf16)
    out[...] = (x[...].astype(f32) + mm(mix, back[...], 0, 0)).astype(out.dtype)


def combine(slot, ids, scores, x, back, base, slots, dtype):
    whole = lambda a: pl.BlockSpec(a.shape, lambda i: (0,) * a.ndim)
    return pl.pallas_call(
        functools.partial(combine_kernel, base=base, slots=slots),
        name="combine",
        grid=(1,),
        in_specs=[whole(a) for a in (slot, ids, scores, x, back)],
        out_specs=whole(x),
        out_shape=jax.ShapeDtypeStruct(x.shape, dtype),
    )(slot, ids, scores, x, back)


def local(
    queries,
    keys,
    values,
    branch_gates,
    block_choice,
    norm_gain,
    expert_ids,
    route_scores,
    w_gate_up,
    w_down,
):
    tokens, features = queries.shape
    blocks_here = tokens // BLOCK
    row = lax.axis_index("seq")
    peers = lax.axis_size("seq")
    me = lax.axis_index("exp")
    ring = lax.axis_size("exp")
    hidden = w_down.shape[1]
    half = hidden // ring

    kv = jnp.stack([keys, values])

    across = 2 * 4
    chip = (row % across) // 2
    odd = row % 2

    def shifted(x, by):
        pairs = [(i, i - i % across + (i + 2 * by) % across) for i in range(peers)]
        return lax.ppermute(x, "seq", pairs)

    def swapped(x):
        return lax.ppermute(x, "seq", [(i, i ^ 1) for i in range(peers)])

    above = lax.ppermute(kv, "seq", [(i, i + across) for i in range(peers - across)])
    far = [shifted(jnp.where(chip >= 4 - by, above, kv), by) for by in (1, 2, 3)]
    beside = swapped(jnp.where(odd == 1, above, kv))
    pieces = [kv, *far, beside, *[swapped(x) for x in far]]
    meta = jnp.stack(
        [row]
        + [jnp.int32(d) for d in (0, 2, 4, 6)]
        + [jnp.where(odd == 1, 1, 7)]
        + [d + 2 * odd for d in (1, 3, 5)]
    ).astype(jnp.int32)
    pooled_here = jnp.mean(
        kv.astype(f32).reshape(2, blocks_here, BLOCK, features), axis=2
    ).astype(bf16)
    copies = jnp.broadcast_to(pooled_here, (peers, *pooled_here.shape))
    everyone = lax.all_to_all(copies, "seq", split_axis=0, concat_axis=0, tiled=True)
    pooled = jnp.transpose(everyone, (1, 0, 2, 3)).reshape(2, peers * blocks_here, features)
    chosen = jnp.repeat(block_choice, BLOCK, axis=0)
    gates = branch_gates.reshape(tokens, -1)
    w_up = jnp.transpose(w_gate_up[0], (1, 2, 0))
    gain = norm_gain[None, :]
    bias, cbias, onehot, slot = tables(
        meta, chosen, expert_ids.T, len(pieces), pooled.shape[1], PARTS, peers
    )
    att, *xs = attention(bias, cbias, onehot, gates, queries, pieces, pooled, PARTS, peers)

    def exchanged(x, n):
        return lax.all_to_all(
            x.reshape(peers, n, features), "seq", split_axis=0, concat_axis=0, tiled=True
        ).reshape(peers * n, features)

    to_right = [(i, (i + 1) % ring) for i in range(ring)]
    to_left = [(i, (i - 1) % ring) for i in range(ring)]
    send_right = lambda x: lax.ppermute(x, "exp", to_right)
    send_left = lambda x: lax.ppermute(x, "exp", to_left)
    order = [0, -1, -2, -3, 1, 2, 3, 4]
    places = jnp.stack([(me + k) % ring for k in order]).astype(jnp.int32)
    middle = half // 2
    summed = []
    for x, n in zip(xs, PARTS):
        whole = project(gain, exchanged(x, n), w_up, ring)
        summed.append(
            lax.psum_scatter(whole.reshape(-1, peers * n), "exp", scatter_dimension=0, tiled=True)
        )
    mixed = att
    base = 0
    for c, n in enumerate(PARTS):
        act = activate(summed[c], half)
        rights, lefts = [act], [act]
        for _ in range(3):
            rights.append(send_right(rights[-1]))
            lefts.append(send_left(lefts[-1]))
        top, bottom = send_right(rights[-1][:middle]), send_left(lefts[-1][middle:])
        if c == 0:
            result = down(places, [*rights, *lefts[1:], top, bottom], w_down[0])
        else:
            near = [*rights[:3], *lefts[1:3]]
            result = down_some(places, near, w_down[0], (0, 1, 2, 4, 5))
            last_blocks = [rights[3], lefts[3], top, bottom]
            result = down_some(places, last_blocks, w_down[0], (3, 6, 7), result)
        back = exchanged(result, n)
        last = c == len(PARTS) - 1
        mixed = combine(
            slot, expert_ids.T, route_scores.T, mixed, back, base, n, bf16 if last else f32
        )
        base += n
    return mixed


def solution(mesh):
    placed = (
        P("seq", "exp"),
        P("seq", "exp"),
        P("seq", "exp"),
        P("seq", None, "exp"),
        P("seq", None),
        P("exp"),
        P("seq", None),
        P("seq", None),
        P("seq", "exp", None, None),
        P("seq", None, "exp"),
    )

    return jax.shard_map(
        local, mesh=mesh, in_specs=placed, out_specs=P("seq", "exp"), check_vma=False
    )
```
